32 devices in a mesh: dp: 16 (over z, x, core), tensor: 2 (over y).
Axes of the slice: x: 2, y: 2, z: 4, core: 2. Of those that a mesh axis runs over, the one named last changes fastest.
Arguments:
- tokens: bfloat16 [16384, 1024], P(('dp', 'tensor')), may hold values from -6 to 6
- cotangent: bfloat16 [16384, 1024], P(('dp', 'tensor')), may hold values from -6 to 6
- segment_ids: int32 [16, 1024], P('dp'), may hold values from 0 to 16, as said below
- w_qkv: float32 [3, 1024, 1024], P(None, 'dp', 'tensor'), may hold values from -0.1875 to 0.1875
- m_qkv: float32 [3, 1024, 1024], P(None, 'dp', 'tensor'), may hold values from -384 to 384
- a_qkv: float32 [3, 1024, 1024], P(None, 'dp', 'tensor'), may hold values from -0.1875 to 0.1875
- w_bqv: float32 [2, 1024], P(None, 'tensor'), may hold values from -6 to 6
- m_bqv: float32 [2, 1024], P(None, 'tensor'), may hold values from -768 to 768
- a_bqv: float32 [2, 1024], P(None, 'tensor'), may hold values from -6 to 6
- w_out: float32 [1024, 1024], P('tensor', 'dp'), may hold values from -1.5 to 1.5
- m_out: float32 [1024, 1024], P('tensor', 'dp'), may hold values from -80 to 80
- a_out: float32 [1024, 1024], P('tensor', 'dp'), may hold values from -1.5 to 1.5
- w_up: float32 [1024, 4096], P('dp', 'tensor'), may hold values from -0.1875 to 0.1875
- m_up: float32 [1024, 4096], P('dp', 'tensor'), may hold values from -224 to 224
- a_up: float32 [1024, 4096], P('dp', 'tensor'), may hold values from -0.1875 to 0.1875
- w_bup: float32 [4096], P('tensor'), may hold values from -6 to 6
- m_bup: float32 [4096], P('tensor'), may hold values from -224 to 224
- a_bup: float32 [4096], P('tensor'), may hold values from -6 to 6
- w_down: float32 [4096, 1024], P('tensor', 'dp'), may hold values from -0.09375 to 0.09375
- m_down: float32 [4096, 1024], P('tensor', 'dp'), may hold values from -384 to 384
- a_down: float32 [4096, 1024], P('tensor', 'dp'), may hold values from -0.09375 to 0.09375
- w_vec: float32 [6, 1024], replicated
- m_vec: float32 [6, 1024], replicated, may hold values from -768 to 768
- a_vec: float32 [6, 1024], replicated
Outputs:
- layer_out: bfloat16 [16384, 1024], P(('dp', 'tensor'))
- grad_tokens: bfloat16 [16384, 1024], P(('dp', 'tensor'))
- newm_qkv: float32 [3, 1024, 1024], P(None, 'dp', 'tensor')
- neww_qkv: float32 [3, 1024, 1024], P(None, 'dp', 'tensor')
- newa_qkv: float32 [3, 1024, 1024], P(None, 'dp', 'tensor')
- newm_bqv: float32 [2, 1024], P(None, 'tensor')
- neww_bqv: float32 [2, 1024], P(None, 'tensor')
- newa_bqv: float32 [2, 1024], P(None, 'tensor')
- newm_out: float32 [1024, 1024], P('tensor', 'dp')
- neww_out: float32 [1024, 1024], P('tensor', 'dp')
- newa_out: float32 [1024, 1024], P('tensor', 'dp')
- newm_up: float32 [1024, 4096], P('dp', 'tensor')
- neww_up: float32 [1024, 4096], P('dp', 'tensor')
- newa_up: float32 [1024, 4096], P('dp', 'tensor')
- newm_bup: float32 [4096], P('tensor')
- neww_bup: float32 [4096], P('tensor')
- newa_bup: float32 [4096], P('tensor')
- newm_down: float32 [4096, 1024], P('tensor', 'dp')
- neww_down: float32 [4096, 1024], P('tensor', 'dp')
- newa_down: float32 [4096, 1024], P('tensor', 'dp')
- newm_vec: float32 [6, 1024], replicated
- neww_vec: float32 [6, 1024], replicated
- newa_vec: float32 [6, 1024], replicated
The draws below stay inside these ranges and needn't reach their ends.
Inputs may be any that keep to these rules, and one draw needn't show every extreme that they name: `segment_ids`: within each sequence the ids start at 0 and rise by one where a document ends; every document has 60 to 800 tokens; some document has exactly 800, and some sequence reaches the largest id.
All inputs are finite; a program needn't handle non-finite values.
Results may differ from the reference program's by a relative error of at most 0.015.
Values may be sent and summed in bfloat16 or wider, within the bound.
No kernel may reach another device: no remote copies, remote signals or barrier semaphores. Data moves between devices by JAX's collectives and lax.ppermute only.
A program may use at most 192 MiB of HBM per device.

```python
import math
import jax
import jax.numpy as jnp
from jax import lax

D = 1024
HEADS = 16
HEAD_DIM = 64
FF = 4096
SEQ_LEN = 1024
QBLOCK = 512
DOC_MIN = 60
DOC_MAX = 800
SEQUENCES = 16
TOKENS = 16384


def vector_rows(key):
    keys = jax.random.split(key, 2)
    base = jax.random.normal(keys[0], (6, D), jnp.float32)
    gains = 1.0 + 0.25 * jax.random.uniform(keys[1], (6, D), jnp.float32, -1.0, 1.0)
    row_index = lax.broadcasted_iota(jnp.int32, (6, D), 0)
    is_gain = (row_index == 2) | (row_index == 4)
    return jnp.where(is_gain, gains, 0.3 * base)


def draw_w_vec(key, part):
    return vector_rows(jax.random.fold_in(key, 11))


def draw_a_vec(key, part):
    return vector_rows(jax.random.fold_in(key, 23))


def draw_segment_ids(key, part):
    doc_count = SEQ_LEN // DOC_MIN + 1
    doc_span = DOC_MAX - DOC_MIN
    keys = jax.random.split(jax.random.fold_in(key, 5), 4)
    doc_lengths = jax.random.randint(keys[0], (SEQUENCES, doc_count), DOC_MIN, doc_span + 1)
    forced = jax.random.randint(keys[1], (SEQUENCES, 1), 0, 2)
    chosen = jax.random.randint(keys[2], (), 0, SEQUENCES)
    short_seq = (chosen + 1) % SEQUENCES
    seq_index = lax.broadcasted_iota(jnp.int32, (SEQUENCES, 1), 0)
    forced = jnp.maximum(forced, (seq_index == chosen).astype(jnp.int32))
    forced = jnp.where(seq_index == short_seq, 0, forced)
    doc_index = lax.broadcasted_iota(jnp.int32, (SEQUENCES, doc_count), 1)
    doc_lengths = jnp.where((doc_index == 0) & (forced == 1), DOC_MAX, doc_lengths)
    doc_lengths = jnp.where(seq_index == short_seq, DOC_MIN, doc_lengths)
    doc_ends = jnp.cumsum(doc_lengths, axis=1)
    usable = doc_ends <= SEQ_LEN - DOC_MIN
    mirror = jax.random.randint(keys[3], (SEQUENCES, 1, 1), 0, 2)
    position = lax.broadcasted_iota(jnp.int32, (SEQUENCES, 1, SEQ_LEN), 2)
    end_cube = doc_ends[:, :, None]
    ahead_hit = end_cube <= position
    behind_hit = end_cube >= SEQ_LEN - position
    crossed = jnp.where(mirror == 1, behind_hit, ahead_hit) & usable[:, :, None]
    return jnp.sum(crossed.astype(jnp.int32), axis=1)


def block_levels(rng, shape, shards, least, largest):
    loudness, own = 1.0, jax.random.fold_in(rng, 6)
    for dim, blocks in shards:
        draws = jnp.exp(jax.random.uniform(jax.random.fold_in(own, dim), (blocks,), jnp.float32, least / len(shards), largest / len(shards)))
        loudness = loudness * jnp.repeat(draws, shape[dim] // blocks).reshape([-1 if axis == dim else 1 for axis in range(len(shape))])
    return loudness


def normal_values(key, extent, width, reach, shards=(), kind=jnp.bfloat16):
    array = width * jax.random.normal(key, extent, jnp.float32)
    if shards:
        array = array * block_levels(key, extent, shards, -0.22, 0.18)
    return jnp.clip(array, -reach, reach).astype(kind)


def setup_inputs(seed: int = 0) -> dict:
    seeds = jax.random.split(jax.random.key(seed), 25)
    tokens = normal_values(seeds[0], (TOKENS, D), 1.0, 6.0, ((0, 32),))
    cotangent = normal_values(seeds[1], (TOKENS, D), 1.0, 6.0, ((0, 32),))
    segment_ids = draw_segment_ids(jax.random.fold_in(seeds[24], 71), 0)
    w_qkv = normal_values(seeds[3], (3, D, D), D ** -0.5, 0.1875, ((1, 16), (2, 2)), jnp.float32)
    m_qkv = normal_values(seeds[4], (3, D, D), (0.5 * TOKENS ** 0.5), 384.0, ((1, 16), (2, 2)), jnp.float32)
    a_qkv = normal_values(seeds[5], (3, D, D), D ** -0.5, 0.1875, ((1, 16), (2, 2)), jnp.float32)
    w_bqv = normal_values(seeds[6], (2, D), 0.5, 6.0, ((1, 2),), jnp.float32)
    m_bqv = normal_values(seeds[7], (2, D), (TOKENS ** 0.5), 768.0, ((1, 2),), jnp.float32)
    a_bqv = normal_values(seeds[8], (2, D), 0.5, 6.0, ((1, 2),), jnp.float32)
    w_out = normal_values(seeds[9], (D, D), (D // 64) ** -0.5, 1.5, ((0, 2), (1, 16)), jnp.float32)
    m_out = normal_values(seeds[10], (D, D), (0.1 * TOKENS ** 0.5), 80.0, ((0, 2), (1, 16)), jnp.float32)
    a_out = normal_values(seeds[11], (D, D), (D // 64) ** -0.5, 1.5, ((0, 2), (1, 16)), jnp.float32)
    w_up = normal_values(seeds[12], (D, FF), D ** -0.5, 0.1875, ((0, 16), (1, 2)), jnp.float32)
    m_up = normal_values(seeds[13], (D, FF), (0.3 * TOKENS ** 0.5), 224.0, ((0, 16), (1, 2)), jnp.float32)
    a_up = normal_values(seeds[14], (D, FF), D ** -0.5, 0.1875, ((0, 16), (1, 2)), jnp.float32)
    w_bup = normal_values(seeds[15], (FF,), 0.5, 6.0, ((0, 2),), jnp.float32)
    m_bup = normal_values(seeds[16], (FF,), (0.3 * TOKENS ** 0.5), 224.0, ((0, 2),), jnp.float32)
    a_bup = normal_values(seeds[17], (FF,), 0.5, 6.0, ((0, 2),), jnp.float32)
    w_down = normal_values(seeds[18], (FF, D), FF ** -0.5, 0.09375, ((0, 2), (1, 16)), jnp.float32)
    m_down = normal_values(seeds[19], (FF, D), (0.5 * TOKENS ** 0.5), 384.0, ((0, 2), (1, 16)), jnp.float32)
    a_down = normal_values(seeds[20], (FF, D), FF ** -0.5, 0.09375, ((0, 2), (1, 16)), jnp.float32)
    w_vec = draw_w_vec(jax.random.fold_in(seeds[24], 71), 0)
    m_vec = normal_values(seeds[22], (6, D), (TOKENS ** 0.5), 768.0, (), jnp.float32)
    a_vec = draw_a_vec(jax.random.fold_in(seeds[24], 71), 0)
    return dict(tokens=tokens, cotangent=cotangent, segment_ids=segment_ids, w_qkv=w_qkv, m_qkv=m_qkv, a_qkv=a_qkv, w_bqv=w_bqv, m_bqv=m_bqv, a_bqv=a_bqv, w_out=w_out, m_out=m_out, a_out=a_out, w_up=w_up, m_up=m_up, a_up=a_up, w_bup=w_bup, m_bup=m_bup, a_bup=a_bup, w_down=w_down, m_down=m_down, a_down=a_down, w_vec=w_vec, m_vec=m_vec, a_vec=a_vec)


NORM_EPS = 1e-05
MOMENTUM = 0.9
AVERAGE = 0.75
MATRIX_RATE = 0.05
FASTER_RATE = 0.25
HIGHEST = lax.Precision.HIGHEST

@jax.custom_vjp
def low(v):
    return lax.optimization_barrier(v.astype(jnp.bfloat16)).astype(jnp.float32)

@jax.custom_vjp
def low_back(v):
    return v

def low_keep(v):
    return (low(v), None)

def low_pass(kept, grad):
    return (grad,)

def back_keep(v):
    return (v, None)

def back_low(kept, grad):
    return (low(grad),)
low.defvjp(low_keep, low_pass)
low_back.defvjp(back_keep, back_low)

def matmul(left, right):
    return jnp.dot(left, right, precision=HIGHEST, preferred_element_type=jnp.float32)

def layer_norm(values, gain, shift):
    centred = values - lax.optimization_barrier(jnp.mean(values, axis=-1, keepdims=True))
    spread = lax.optimization_barrier(jnp.mean(centred * centred, axis=-1, keepdims=True))
    return centred * lax.rsqrt(spread + NORM_EPS) * gain + shift

def attend(query, key_rows, value_rows, segments):
    seq_count = segments.shape[0]
    shaped = (seq_count, SEQ_LEN, HEADS, HEAD_DIM)
    query_heads = query.reshape(shaped)
    key_heads = key_rows.reshape(shaped)
    value_heads = value_rows.reshape(shaped)
    score_scale = HEAD_DIM ** (-0.5)

    def one_block(block_index):
        start = block_index * QBLOCK
        query_block = lax.dynamic_slice_in_dim(query_heads, start, QBLOCK, 1)
        row_segments = lax.dynamic_slice_in_dim(segments, start, QBLOCK, 1)
        scores = low_back(jnp.einsum('bqhd,bkhd->bhqk', query_block, key_heads, precision=HIGHEST) * score_scale)
        same_doc = row_segments[:, None, :, None] == segments[:, None, None, :]
        probs = low(jax.nn.softmax(jnp.where(same_doc, scores, -1e+30), axis=-1))
        return jnp.einsum('bhqk,bkhd->bqhd', probs, value_heads, precision=HIGHEST)
    blocks = lax.map(jax.checkpoint(one_block), jnp.arange(SEQ_LEN // QBLOCK, dtype=jnp.int32))
    return jnp.moveaxis(blocks, 0, 1).reshape(seq_count * SEQ_LEN, HEADS * HEAD_DIM)

def forward(token_rows, segments, w_qkv, w_bqv, w_out, w_up, w_bup, w_down, w_vec):
    qkv16 = low(w_qkv)
    query = low(low_back(matmul(token_rows, qkv16[0])) + w_bqv[0])
    key_rows = low(low_back(matmul(token_rows, qkv16[1])))
    value_rows = low(low_back(matmul(token_rows, qkv16[2])) + w_bqv[1])
    context = low(low_back(attend(query, key_rows, value_rows, segments)))
    attended = low_back(matmul(context, low(w_out))) + w_vec[0]
    hidden = layer_norm(token_rows + attended, w_vec[2], w_vec[3])
    upper = low_back(matmul(low(hidden), low(w_up))) + w_bup
    active = low(jax.nn.gelu(upper, approximate=False))
    mixed = low_back(matmul(active, low(w_down))) + w_vec[1]
    return layer_norm(hidden + mixed, w_vec[4], w_vec[5])

def advance(weight, moment, average, gradient, step_rate):
    new_moment = MOMENTUM * moment + gradient
    new_weight = weight - step_rate * (gradient + MOMENTUM * new_moment)
    new_average = AVERAGE * average + (1.0 - AVERAGE) * new_weight
    return (new_moment, new_weight, new_average)

def reference(tokens, cotangent, segment_ids, w_qkv, m_qkv, a_qkv, w_bqv, m_bqv, a_bqv, w_out, m_out, a_out, w_up, m_up, a_up, w_bup, m_bup, a_bup, w_down, m_down, a_down, w_vec, m_vec, a_vec):
    per_block = math.gcd(SEQUENCES, max(1, 4096 // SEQ_LEN))
    block_count = SEQUENCES // per_block
    token_blocks = tokens.astype(jnp.float32).reshape(block_count, per_block * SEQ_LEN, D)
    back_blocks = cotangent.astype(jnp.float32).reshape(block_count, per_block * SEQ_LEN, D)
    segment_blocks = segment_ids.reshape(block_count, per_block, SEQ_LEN)
    params = (w_qkv, w_bqv, w_out, w_up, w_bup, w_down, w_vec)

    def one_step(totals, inputs):
        block_rows, block_back, block_segments = inputs

        def apply_layer(values, *weights):
            return forward(values, block_segments, *weights)
        output, pull = jax.vjp(apply_layer, block_rows, *params)
        gradients = pull(block_back)
        totals = tuple((total + grad for total, grad in zip(totals, gradients[1:])))
        return (totals, (output.astype(jnp.bfloat16), gradients[0].astype(jnp.bfloat16)))
    start_totals = tuple((jnp.zeros(param.shape, jnp.float32) for param in params))
    totals, (outputs, input_grads) = lax.scan(one_step, start_totals, (token_blocks, back_blocks, segment_blocks))
    base_rate = 1.0 / math.sqrt(TOKENS)
    slow_rate = MATRIX_RATE * base_rate
    fast_rate = FASTER_RATE * base_rate
    nm_qkv, nw_qkv, na_qkv = advance(w_qkv, m_qkv, a_qkv, totals[0], slow_rate)
    nm_bqv, nw_bqv, na_bqv = advance(w_bqv, m_bqv, a_bqv, totals[1], slow_rate)
    nm_out, nw_out, na_out = advance(w_out, m_out, a_out, totals[2], fast_rate)
    nm_up, nw_up, na_up = advance(w_up, m_up, a_up, totals[3], slow_rate)
    nm_bup, nw_bup, na_bup = advance(w_bup, m_bup, a_bup, totals[4], fast_rate)
    nm_down, nw_down, na_down = advance(w_down, m_down, a_down, totals[5], slow_rate)
    nm_vec, nw_vec, na_vec = advance(w_vec, m_vec, a_vec, totals[6], slow_rate)
    return (outputs.reshape(TOKENS, D), input_grads.reshape(TOKENS, D), nm_qkv, nw_qkv, na_qkv, nm_bqv, nw_bqv, na_bqv, nm_out, nw_out, na_out, nm_up, nw_up, na_up, nm_bup, nw_bup, na_bup, nm_down, nw_down, na_down, nm_vec, nw_vec, na_vec)
```

```python
import math

import jax
import jax.numpy as jnp
from jax import lax
from jax.sharding import Mesh, PartitionSpec as P

HEAD_DIM = 64
SEQ_LEN = 1024
SEQ_GRP = 1
QBLOCK = 512


NORM_EPS = 1e-05
MOMENTUM = 0.9
AVERAGE = 0.75
MATRIX_RATE = 0.05
FASTER_RATE = 0.25


def layer_norm(values, gain, shift):
    centred = values - jnp.mean(values, axis=-1, keepdims=True)
    spread = jnp.mean(centred * centred, axis=-1, keepdims=True)
    return centred * lax.rsqrt(spread + NORM_EPS) * gain + shift


def gelu_exact(values):
    return jax.nn.gelu(values, approximate=False)


def advance(weight, moment, average, gradient, step_rate):
    new_moment = MOMENTUM * moment + gradient
    new_weight = weight - step_rate * (gradient + MOMENTUM * new_moment)
    new_average = AVERAGE * average + (1.0 - AVERAGE) * new_weight
    return (new_moment, new_weight, new_average)


def attend_forward(packed, segment_ids):
    seq_count, length = segment_ids.shape
    blocks_per = length // QBLOCK
    dev_width = packed.shape[2]
    local_heads = dev_width // HEAD_DIM
    score_scale = HEAD_DIM ** (-0.5)
    shaped = packed.reshape(3, seq_count, length, local_heads, HEAD_DIM)

    def one_sequence(inputs):
        query_all, key_all, value_all, seg_all = inputs

        def one_block(block_index):
            start = block_index * QBLOCK
            query_rows = lax.dynamic_slice_in_dim(query_all, start, QBLOCK, 0)
            row_seg = lax.dynamic_slice_in_dim(seg_all, start, QBLOCK, 0)
            scores = (
                jnp.einsum("qhd,khd->hqk", query_rows, key_all, preferred_element_type=jnp.float32)
                * score_scale
            )
            same_doc = (row_seg[:, None] == seg_all[None, :])[None]
            scores = jnp.where(same_doc, scores, -1e30)
            row_max = jnp.max(scores, axis=-1, keepdims=True)
            exp_scores = jnp.exp(scores - row_max)
            row_total = jnp.sum(exp_scores, axis=-1, keepdims=True)
            probs16 = (exp_scores / row_total).astype(jnp.bfloat16)
            context = jnp.einsum(
                "hqk,khd->qhd", probs16, value_all, preferred_element_type=jnp.float32
            )
            return (
                context.astype(jnp.bfloat16).reshape(QBLOCK, dev_width),
                (row_max + jnp.log(row_total))[..., 0],
            )

        context, logsum = lax.map(one_block, jnp.arange(blocks_per, dtype=jnp.int32))
        return (context.reshape(length, dev_width), logsum)

    context, logsum = lax.map(one_sequence, (shaped[0], shaped[1], shaped[2], segment_ids))
    return (context.reshape(seq_count * length, dev_width), logsum)


def attend_backward(packed, context_grad, logsum, segment_ids):
    seq_count, length = segment_ids.shape
    blocks_per = length // QBLOCK
    dev_width = packed.shape[2]
    local_heads = dev_width // HEAD_DIM
    score_scale = HEAD_DIM ** (-0.5)
    shaped = packed.reshape(3, seq_count, length, local_heads, HEAD_DIM)
    grad_shaped = context_grad.reshape(seq_count, length, local_heads, HEAD_DIM)

    def one_sequence(inputs):
        query_all, key_all, value_all, grad_all, lse_all, seg_all = inputs

        def one_block(carry, block_index):
            key_grad, value_grad = carry
            start = block_index * QBLOCK
            query_rows = lax.dynamic_slice_in_dim(query_all, start, QBLOCK, 0)
            grad_rows = lax.dynamic_slice_in_dim(grad_all, start, QBLOCK, 0)
            row_seg = lax.dynamic_slice_in_dim(seg_all, start, QBLOCK, 0)
            row_lse = lax.dynamic_index_in_dim(lse_all, block_index, 0, keepdims=False)
            scores = (
                jnp.einsum("qhd,khd->hqk", query_rows, key_all, preferred_element_type=jnp.float32)
                * score_scale
            )
            same_doc = (row_seg[:, None] == seg_all[None, :])[None]
            probs = jnp.where(same_doc, jnp.exp(scores - row_lse[..., None]), 0.0)
            value_grad = value_grad + jnp.einsum(
                "hqk,qhd->khd",
                probs.astype(jnp.bfloat16),
                grad_rows,
                preferred_element_type=jnp.float32,
            )
            prob_grad = jnp.einsum(
                "qhd,khd->hqk", grad_rows, value_all, preferred_element_type=jnp.float32
            )
            inner_sum = jnp.sum(probs * prob_grad, axis=-1, keepdims=True)
            score_grad = (probs * (prob_grad - inner_sum)).astype(jnp.bfloat16)
            query_grad = (
                jnp.einsum("hqk,khd->qhd", score_grad, key_all, preferred_element_type=jnp.float32)
                * score_scale
            )
            key_grad = (
                key_grad
                + jnp.einsum(
                    "hqk,qhd->khd", score_grad, query_rows, preferred_element_type=jnp.float32
                )
                * score_scale
            )
            return ((key_grad, value_grad), query_grad)

        zero_grad = jnp.zeros(key_all.shape, jnp.float32)
        (key_grad, value_grad), query_grad = lax.scan(
            one_block, (zero_grad, zero_grad), jnp.arange(blocks_per, dtype=jnp.int32)
        )
        return (query_grad.reshape(key_all.shape), key_grad, value_grad)

    query_grad, key_grad, value_grad = lax.map(
        one_sequence, (shaped[0], shaped[1], shaped[2], grad_shaped, logsum, segment_ids)
    )
    total_rows = seq_count * length
    return jnp.stack(
        [
            query_grad.reshape(total_rows, dev_width),
            key_grad.reshape(total_rows, dev_width),
            value_grad.reshape(total_rows, dev_width),
        ]
    )

SWAP = [(core * 2 + side, side * 2 + core) for core in range(2) for side in range(2)]
FLIP = [(0, 1), (1, 0)]


def swap(values):
    return lax.ppermute(values, ("core", "tensor"), SWAP)


def core_exchange(values):
    return lax.ppermute(values, "core", FLIP)


def y_exchange(values):
    return lax.ppermute(values, "tensor", FLIP)


def chip_exchange(values, mask):
    count = lax.axis_size("chip")
    return lax.ppermute(values, "chip", [(k, k ^ mask) for k in range(count)])


def bits():
    chip = lax.axis_index("chip")
    return (lax.axis_index("tensor"), chip & 1, (chip >> 1) & 1, (chip >> 2) & 1)


STAGES = (
    y_exchange,
    lambda values: chip_exchange(values, 1),
    lambda values: chip_exchange(values, 2),
    lambda values: chip_exchange(values, 4),
)
Y, X, Z1, Z2 = range(4)


def join(mine, stage, axis):
    other = STAGES[stage](mine)
    first = bits()[stage] == 0
    return jnp.where(
        first, jnp.stack([mine, other], axis), jnp.stack([other, mine], axis)
    )


def gather_pair(left, right):
    rows, width = left.shape
    if lax.axis_size("chip") != 8:
        return tuple(
            lax.all_gather(part, ("chip", "tensor"), axis=0, tiled=True) for part in (left, right)
        )
    both = jnp.stack([left, right])
    both = join(both, Z1, 1)
    both = join(both, Z2, 1)
    left = join(join(both[0], X, 2), Y, 3)
    right = join(join(both[1], Y, 2), X, 2)
    return (left.reshape(16 * rows, width), right.reshape(16 * rows, width))


def split(values, stage, axis):
    bit = bits()[stage]
    keep = lax.dynamic_index_in_dim(values, bit, axis, keepdims=False)
    send = lax.dynamic_index_in_dim(values, 1 - bit, axis, keepdims=False)
    other = STAGES[stage](send)
    return (keep.astype(jnp.float32) + other.astype(jnp.float32)).astype(values.dtype)


def reduce_pair(left, right):
    width = left.shape[1]
    if lax.axis_size("chip") != 8:
        left, right = tuple(
            lax.psum_scatter(part, ("chip", "tensor"), scatter_dimension=0, tiled=True)
            for part in (left, right)
        )
        both = jnp.stack([left, right])
    else:
        left = left.reshape(2, 2, 2, 2, -1, width)
        right = right.reshape(2, 2, 2, 2, -1, width)
        left = split(split(left, Y, 3), X, 2)
        right = split(split(right, X, 2), Y, 2)
        both = jnp.stack([left, right])
        both = split(split(both, Z2, 1), Z1, 1)
    both = swap(both)
    return (both[0].astype(jnp.float32), both[1].astype(jnp.float32))


def sum_all(values):
    if lax.axis_size("chip") != 8:
        return lax.psum(values, ("chip", "tensor"))
    for stage in (Y, X, Z1, Z2):
        values = values + STAGES[stage](values)
    return values


def body(
    tokens,
    cotangent,
    segment_ids,
    w_qkv,
    m_qkv,
    a_qkv,
    w_bqv,
    m_bqv,
    a_bqv,
    w_out,
    m_out,
    a_out,
    w_up,
    m_up,
    a_up,
    w_bup,
    m_bup,
    a_bup,
    w_down,
    m_down,
    a_down,
    w_vec,
    m_vec,
    a_vec,
):
    f32, bf16 = jnp.float32, jnp.bfloat16
    core = lax.axis_index("core")
    dev_width = w_bqv.shape[1]
    unit_width = w_bup.shape[0]
    rows = tokens.shape[0]
    half = dev_width // 2
    tokens = swap(tokens)
    qkv_shard = w_qkv.astype(bf16)
    qkv_halves = swap(
        jnp.stack([jnp.concatenate([qkv_shard[k, :, h * half : (h + 1) * half] for k in range(3)], 1) for h in range(2)])
    )
    segments = swap(segment_ids)
    biases = swap(jnp.concatenate([w_bqv.reshape(-1), w_bup]))
    b_qv = biases[: 2 * dev_width].reshape(2, dev_width)
    b_up = biases[2 * dev_width :]
    out_shard = w_out.T.astype(bf16)
    up_shard = w_up.astype(bf16)
    down_shard = w_down.T.astype(bf16)
    up_out = swap(
        jnp.stack(
            [
                jnp.concatenate([out_shard[:, h * half : (h + 1) * half], up_shard[:, h * unit_width // 2 : (h + 1) * unit_width // 2]], 1)
                for h in range(2)
            ]
        )
    )
    down_halves = swap(
        jnp.stack([down_shard[:, h * unit_width // 2 : (h + 1) * unit_width // 2] for h in range(2)])
    )
    cotangent = swap(cotangent)
    tok_full = jnp.concatenate([tokens, core_exchange(tokens)])
    segments = jnp.where(core == 1, jnp.roll(segments, rows, axis=1), segments)
    qkv_a, qkv_b = gather_pair(qkv_halves[0], qkv_halves[1])
    uo_a, uo_b = gather_pair(up_out[0], up_out[1])
    down_a, down_b = gather_pair(down_halves[0], down_halves[1])
    qkv16 = jnp.stack(
        [jnp.concatenate([part[:, k * half : (k + 1) * half] for part in (qkv_a, qkv_b)], 1) for k in range(3)]
    )
    out_t = jnp.concatenate([uo_a[:, :half], uo_b[:, :half]], 1)
    up16 = jnp.concatenate([uo_a[:, half:], uo_b[:, half:]], 1)
    down_t = jnp.concatenate([down_a, down_b], 1)

    bias_rows = jnp.stack([b_qv[0], jnp.zeros_like(b_qv[0]), b_qv[1]])[:, None, :]
    packed = (
        jnp.einsum("nd,kde->kne", tok_full, qkv16, preferred_element_type=f32) + bias_rows
    ).astype(bf16)
    context, logsum = attend_forward(packed, segments)

    def summed(left, right, form):
        away = jnp.einsum(form, left[rows:], right, preferred_element_type=f32)
        other = core_exchange(away.astype(bf16))
        return jnp.einsum(form, left[:rows], right, preferred_element_type=f32) + other.astype(f32)

    attended = summed(context, out_t, "ne,de->nd")
    first_sum = tokens.astype(f32) + attended + w_vec[0]
    hidden, first_pull = jax.vjp(layer_norm, first_sum, w_vec[2], w_vec[3])
    hidden16 = hidden.astype(bf16)
    hidden_full = jnp.concatenate([hidden16, core_exchange(hidden16)])
    upper = jnp.dot(hidden_full, up16, preferred_element_type=f32) + b_up
    active, gelu_pull = jax.vjp(gelu_exact, upper)
    active16 = active.astype(bf16)
    mixed = summed(active16, down_t, "nf,df->nd")
    second_sum = hidden + mixed + w_vec[1]
    normed, second_pull = jax.vjp(layer_norm, second_sum, w_vec[4], w_vec[5])
    layer_out = swap(normed.astype(bf16))
    second_grad, gain2_grad, shift2_grad = second_pull(cotangent.astype(f32))
    second16 = second_grad.astype(bf16)
    mixed_full = jnp.concatenate([second16, core_exchange(second16)])
    active_grad = jnp.einsum("nd,df->nf", mixed_full, down_t, preferred_element_type=f32)
    down_grad = jnp.einsum("nd,nf->df", mixed_full, active16, preferred_element_type=f32).astype(bf16)
    upper_grad = gelu_pull(active_grad)[0]
    upper16 = upper_grad.astype(bf16)
    up_grad = jnp.einsum("nd,nf->df", hidden_full, upper16, preferred_element_type=f32).astype(bf16)
    hidden_grad = second_grad + summed(upper16, up16, "nf,df->nd")
    first_grad, gain1_grad, shift1_grad = first_pull(hidden_grad)
    first16 = first_grad.astype(bf16)
    attended_full = jnp.concatenate([first16, core_exchange(first16)])
    context_grad = jnp.einsum("nd,de->ne", attended_full, out_t, preferred_element_type=f32).astype(bf16)
    out_grad = jnp.einsum("nd,ne->de", attended_full, context, preferred_element_type=f32).astype(bf16)
    packed_grad = attend_backward(packed, context_grad, logsum, segments)
    bqv_local = jnp.stack([jnp.sum(packed_grad[0], axis=0), jnp.sum(packed_grad[2], axis=0)])
    packed16 = packed_grad.astype(bf16)
    qkv_grad = jnp.einsum("nd,kne->kde", tok_full, packed16, preferred_element_type=f32).astype(bf16)
    away = jnp.einsum("kne,kde->nd", packed16[:, rows:], qkv16, preferred_element_type=f32)
    other = core_exchange(away.astype(bf16))
    near = jnp.einsum("kne,kde->nd", packed16[:, :rows], qkv16, preferred_element_type=f32)
    grad_tokens = swap((first_grad + near + other.astype(f32)).astype(bf16))

    down_l, down_r = reduce_pair(down_grad[:, : unit_width // 2], down_grad[:, unit_width // 2 :])
    uo_l, uo_r = reduce_pair(
        *(
            jnp.concatenate([out_grad[:, h * half : (h + 1) * half], up_grad[:, h * unit_width // 2 : (h + 1) * unit_width // 2]], 1)
            for h in range(2)
        )
    )
    qkv_l, qkv_r = reduce_pair(
        *(jnp.concatenate([qkv_grad[k, :, h * half : (h + 1) * half] for k in range(3)], 1) for h in range(2))
    )
    qkv_part = jnp.stack(
        [jnp.concatenate([part[:, k * half : (k + 1) * half] for part in (qkv_l, qkv_r)], 1) for k in range(3)]
    )
    out_part = jnp.concatenate([uo_l[:, :half], uo_r[:, :half]], 1).T
    up_part = jnp.concatenate([uo_l[:, half:], uo_r[:, half:]], 1)
    down_part = jnp.concatenate([down_l, down_r], 1).T

    vec_local = jnp.stack(
        [
            jnp.sum(first_grad, axis=0),
            jnp.sum(second_grad, axis=0),
            gain1_grad,
            shift1_grad,
            gain2_grad,
            shift2_grad,
        ]
    )
    vec_local = vec_local + core_exchange(vec_local)
    early = sum_all(jnp.concatenate([vec_local.reshape(-1), jnp.sum(upper_grad, axis=0)]))
    vec_grad = early[: vec_local.size].reshape(vec_local.shape)
    bup_grad = swap(early[vec_local.size :])
    bqv_grad = swap(sum_all(bqv_local))
    base_rate = 1.0 / math.sqrt(SEQ_LEN * lax.axis_size(("chip", "core")))
    slow_rate = MATRIX_RATE * base_rate
    fast_rate = FASTER_RATE * base_rate
    nm_qkv, nw_qkv, na_qkv = advance(w_qkv, m_qkv, a_qkv, qkv_part, slow_rate)
    nm_bqv, nw_bqv, na_bqv = advance(w_bqv, m_bqv, a_bqv, bqv_grad, slow_rate)
    nm_out, nw_out, na_out = advance(w_out, m_out, a_out, out_part, fast_rate)
    nm_up, nw_up, na_up = advance(w_up, m_up, a_up, up_part, slow_rate)
    nm_bup, nw_bup, na_bup = advance(w_bup, m_bup, a_bup, bup_grad, fast_rate)
    nm_down, nw_down, na_down = advance(w_down, m_down, a_down, down_part, slow_rate)
    nm_vec, nw_vec, na_vec = advance(w_vec, m_vec, a_vec, vec_grad, slow_rate)
    return (
        layer_out,
        grad_tokens,
        nm_qkv,
        nw_qkv,
        na_qkv,
        nm_bqv,
        nw_bqv,
        na_bqv,
        nm_out,
        nw_out,
        na_out,
        nm_up,
        nw_up,
        na_up,
        nm_bup,
        nw_bup,
        na_bup,
        nm_down,
        nw_down,
        na_down,
        nm_vec,
        nw_vec,
        na_vec,
    )


def solution(mesh):
    devices = mesh.devices.reshape(-1, 2, 2)
    split_mesh = Mesh(devices, ("chip", "core", "tensor"))
    dp = ("chip", "core")
    row = P(("chip", "core", "tensor"), None)
    deep = P(None, dp, "tensor")
    wide = P("tensor", dp)
    tall = P(dp, "tensor")
    qv = P(None, "tensor")
    unit = P("tensor")
    in_specs = (row, row, P(dp, None)) + (deep,) * 3 + (qv,) * 3 + (wide,) * 3 + (tall,) * 3 + (unit,) * 3 + (wide,) * 3 + (P(),) * 3
    out_specs = (row, row) + in_specs[3:]
    return jax.shard_map(body, mesh=split_mesh, in_specs=in_specs, out_specs=out_specs, check_vma=False)
```

```python
import functools
import math

import jax
import jax.numpy as jnp
from jax import lax
from jax.experimental import pallas as pl
from jax.experimental.pallas import tpu as pltpu
from jax.sharding import Mesh, PartitionSpec as P

HEAD_DIM = 64
SEQ_LEN = 1024


NORM_EPS = 1e-05
MOMENTUM = 0.9
AVERAGE = 0.75
MATRIX_RATE = 0.05
FASTER_RATE = 0.25


def layer_norm(values, gain, shift):
    centred = values - jnp.mean(values, axis=-1, keepdims=True)
    spread = jnp.mean(centred * centred, axis=-1, keepdims=True)
    return centred * lax.rsqrt(spread + NORM_EPS) * gain + shift


def gelu_exact(values):
    return jax.nn.gelu(values, approximate=False)


def advance(weight, moment, average, gradient, step_rate):
    new_moment = MOMENTUM * moment + gradient
    new_weight = weight - step_rate * (gradient + MOMENTUM * new_moment)
    new_average = AVERAGE * average + (1.0 - AVERAGE) * new_weight
    return (new_moment, new_weight, new_average)


NT = (((1,), (1,)), ((), ()))
TN = (((0,), (0,)), ((), ()))
FAR = -1e30


def dot32(left, right, dims=(((1,), (0,)), ((), ()))):
    return lax.dot_general(left, right, dims, preferred_element_type=jnp.float32)


def three_terms(values):
    high = values.astype(jnp.bfloat16).astype(jnp.float32)
    rest = values - high
    middle = rest.astype(jnp.bfloat16).astype(jnp.float32)
    return (high, middle, rest - middle)


def place(lane, terms, other):
    high, middle, low = terms
    return jnp.where(lane == 63, high, jnp.where(lane == 62, middle, jnp.where(lane == 61, low, other)))


def forward_kernel(q_ref, k_ref, v_ref, seg_ref, out_ref, lse_ref, *, block):
    f32, bf16 = jnp.float32, jnp.bfloat16
    rows = q_ref.shape[0]
    lanes = lax.broadcasted_iota(jnp.int32, (rows, 128), 1)
    lower = lanes < HEAD_DIM
    lane = lanes & 63
    same = lane == seg_ref[...]
    q_mark = jnp.where(same, 1.0, 0.0)
    k_mark = jnp.where(same, 0.0, FAR)
    query = q_ref[...].astype(f32)
    keys = k_ref[...].astype(f32) * 0.125
    value = v_ref[...].astype(f32)
    q_heads = [jnp.where(lower, query, q_mark).astype(bf16), jnp.where(lower, q_mark, query).astype(bf16)]
    k_heads = [jnp.where(lower, keys, k_mark).astype(bf16), jnp.where(lower, k_mark, keys).astype(bf16)]
    v_heads = [jnp.where(lower, value, 1.0).astype(bf16), jnp.where(lower, 1.0, value).astype(bf16)]
    low = lower[:block]
    for start in range(0, rows, block):
        parts = []
        for head in range(2):
            scores = dot32(q_heads[head][start : start + block], k_heads[head], NT)
            top = jnp.max(scores, axis=1, keepdims=True)
            weights = jnp.exp(scores - top).astype(bf16)
            parts.append((dot32(weights, v_heads[head]), top))
        (first, top0), (second, top1) = parts
        total = pltpu.roll(jnp.where(low, second, first), HEAD_DIM, 1)
        out_ref[start : start + block, :] = (jnp.where(low, first, second) / total).astype(bf16)
        lse_ref[start : start + block, :] = jnp.where(low, top0, top1) + jnp.log(total)


def backward_kernel(q_ref, k_ref, v_ref, g_ref, o_ref, lse_ref, seg_ref, d_ref, sum_ref, *, block):
    f32, bf16 = jnp.float32, jnp.bfloat16
    rows = q_ref.shape[0]
    lanes = lax.broadcasted_iota(jnp.int32, (rows, 128), 1)
    lower = lanes < HEAD_DIM
    lane = lanes & 63
    same = lane == seg_ref[...]
    query = q_ref[...].astype(f32)
    keys = k_ref[...].astype(f32) * 0.125
    value = v_ref[...].astype(f32)
    grad = g_ref[...].astype(f32)
    lse = pltpu.roll(lse_ref[...], HEAD_DIM, 1)
    q_mark = place(lane, three_terms(-lse), jnp.where(same, 1.0, 0.0))
    k_mark = jnp.where(lane > 60, 1.0, jnp.where(same, 0.0, FAR))
    inner = grad * o_ref[...].astype(f32)
    inner0 = jnp.sum(jnp.where(lower, inner, 0.0), axis=1, keepdims=True)
    inner1 = jnp.sum(jnp.where(lower, 0.0, inner), axis=1, keepdims=True)
    g_mark = place(lane, three_terms(-jnp.where(lower, inner1, inner0)), 0.0)
    v_mark = jnp.where(lane > 60, 1.0, 0.0)

    def heads(values, mark):
        return [jnp.where(lower, values, mark).astype(bf16), jnp.where(lower, mark, values).astype(bf16)]

    q_heads, k_heads = heads(query, q_mark), heads(keys, k_mark)
    v_heads, g_heads = heads(value, v_mark), heads(grad, g_mark)
    q_small = (query * 0.125).astype(bf16)
    k_small = keys.astype(bf16)
    grad16 = g_ref[...]
    low = lower[:block]
    q_grads = [None, None]
    v_sum = jnp.zeros((1, 128), f32)
    for start in range(0, rows, block):
        stop = start + block
        dv, dk = [], []
        for head in range(2):
            probs = jnp.exp(dot32(k_heads[head][start:stop], q_heads[head], NT))
            delta = dot32(v_heads[head][start:stop], g_heads[head], NT)
            dv.append(dot32(probs.astype(bf16), grad16))
            change = (probs * delta).astype(bf16)
            dk.append(dot32(change, q_small))
            part = dot32(change, k_small[start:stop], TN)
            q_grads[head] = part if q_grads[head] is None else q_grads[head] + part
        v_grad = jnp.where(low, dv[0], dv[1])
        v_sum = v_sum + jnp.sum(v_grad, axis=0, keepdims=True)
        d_ref[1, start:stop, :] = jnp.where(low, dk[0], dk[1]).astype(bf16)
        d_ref[2, start:stop, :] = v_grad.astype(bf16)
    q_grad = jnp.where(lower, q_grads[0], q_grads[1])
    d_ref[0] = q_grad.astype(bf16)
    sum_ref[0:1, :] = jnp.sum(q_grad, axis=0, keepdims=True)
    sum_ref[1:2, :] = v_sum


def part_spec(index, rows, base):
    return pl.BlockSpec((None, rows, 128), lambda i: (index, 0, base + i))


def attend_forward(packed, seg_col, base, pairs, block=512):
    rows = packed.shape[1]
    flat = pl.BlockSpec((rows, 128), lambda i: (0, i))
    return pl.pallas_call(
        functools.partial(forward_kernel, block=block),
        grid=(pairs,),
        in_specs=[part_spec(k, rows, base) for k in range(3)] + [pl.BlockSpec((rows, 1), lambda i: (0, 0))],
        out_specs=[flat, flat],
        out_shape=[
            jax.ShapeDtypeStruct((rows, pairs * 128), jnp.bfloat16),
            jax.ShapeDtypeStruct((rows, pairs * 128), jnp.float32),
        ],
        compiler_params=pltpu.CompilerParams(vmem_limit_bytes=48 * 2**20),
        name="attend_forward",
    )(packed, packed, packed, seg_col)


def attend_backward(packed, grad, context, lse, seg_col, base, pairs, block=256):
    rows = packed.shape[1]
    shifted = pl.BlockSpec((rows, 128), lambda i: (0, base + i))
    return pl.pallas_call(
        functools.partial(backward_kernel, block=block),
        grid=(pairs,),
        in_specs=[part_spec(k, rows, base) for k in range(3)] + [shifted] * 3 + [pl.BlockSpec((rows, 1), lambda i: (0, 0))],
        out_specs=[
            pl.BlockSpec((3, rows, 128), lambda i: (0, 0, i)),
            pl.BlockSpec((2, 128), lambda i: (0, i)),
        ],
        out_shape=[
            jax.ShapeDtypeStruct((3, rows, pairs * 128), jnp.bfloat16),
            jax.ShapeDtypeStruct((2, pairs * 128), jnp.float32),
        ],
        compiler_params=pltpu.CompilerParams(vmem_limit_bytes=48 * 2**20),
        name="attend_backward",
    )(packed, packed, packed, grad, context, lse, seg_col)


SWAP = [(core * 2 + side, side * 2 + core) for core in range(2) for side in range(2)]
FLIP = [(0, 1), (1, 0)]


def swap(values):
    return lax.ppermute(values, ("core", "tensor"), SWAP)


def core_exchange(values):
    return lax.ppermute(values, "core", FLIP)


def y_exchange(values):
    return lax.ppermute(values, "tensor", FLIP)


def chip_exchange(values, mask):
    count = lax.axis_size("chip")
    return lax.ppermute(values, "chip", [(k, k ^ mask) for k in range(count)])


def bits():
    chip = lax.axis_index("chip")
    return (lax.axis_index("tensor"), chip & 1, (chip >> 1) & 1, (chip >> 2) & 1)


STAGES = (
    y_exchange,
    lambda values: chip_exchange(values, 1),
    lambda values: chip_exchange(values, 2),
    lambda values: chip_exchange(values, 4),
)
Y, X, Z1, Z2 = range(4)


def join(mine, stage, axis):
    other = STAGES[stage](mine)
    first = bits()[stage] == 0
    return jnp.where(
        first, jnp.stack([mine, other], axis), jnp.stack([other, mine], axis)
    )


def gather_pair(left, right):
    rows, width = left.shape
    if lax.axis_size("chip") != 8:
        return tuple(
            lax.all_gather(part, ("chip", "tensor"), axis=0, tiled=True) for part in (left, right)
        )
    both = jnp.stack([left, right])
    both = join(both, Z1, 1)
    both = join(both, Z2, 1)
    left = join(join(both[0], X, 2), Y, 3)
    right = join(join(both[1], Y, 2), X, 2)
    return (left.reshape(16 * rows, width), right.reshape(16 * rows, width))


def split(values, stage, axis):
    bit = bits()[stage]
    keep = lax.dynamic_index_in_dim(values, bit, axis, keepdims=False)
    send = lax.dynamic_index_in_dim(values, 1 - bit, axis, keepdims=False)
    other = STAGES[stage](send)
    return (keep.astype(jnp.float32) + other.astype(jnp.float32)).astype(values.dtype)


def reduce_pair(left, right):
    width = left.shape[1]
    if lax.axis_size("chip") != 8:
        left, right = tuple(
            lax.psum_scatter(part, ("chip", "tensor"), scatter_dimension=0, tiled=True)
            for part in (left, right)
        )
        both = jnp.stack([left, right])
    else:
        left = left.reshape(2, 2, 2, 2, -1, width)
        right = right.reshape(2, 2, 2, 2, -1, width)
        left = split(split(left, Y, 3), X, 2)
        right = split(split(right, X, 2), Y, 2)
        both = jnp.stack([left, right])
        both = split(split(both, Z2, 1), Z1, 1)
    both = swap(both)
    return (both[0].astype(jnp.float32), both[1].astype(jnp.float32))


def sum_all(values):
    if lax.axis_size("chip") != 8:
        return lax.psum(values, ("chip", "tensor"))
    for stage in (Y, X, Z1, Z2):
        values = values + STAGES[stage](values)
    return values


def body(
    tokens,
    cotangent,
    segment_ids,
    w_qkv,
    m_qkv,
    a_qkv,
    w_bqv,
    m_bqv,
    a_bqv,
    w_out,
    m_out,
    a_out,
    w_up,
    m_up,
    a_up,
    w_bup,
    m_bup,
    a_bup,
    w_down,
    m_down,
    a_down,
    w_vec,
    m_vec,
    a_vec,
):
    f32, bf16 = jnp.float32, jnp.bfloat16
    core = lax.axis_index("core")
    dev_width = w_bqv.shape[1]
    unit_width = w_bup.shape[0]
    rows = tokens.shape[0]
    half = dev_width // 2
    tokens = swap(tokens)
    qkv_shard = w_qkv.astype(bf16)
    qkv_halves = swap(
        jnp.stack([jnp.concatenate([qkv_shard[k, :, h * half : (h + 1) * half] for k in range(3)], 1) for h in range(2)])
    )
    segments = swap(segment_ids)
    biases = swap(jnp.concatenate([w_bqv.reshape(-1), w_bup]))
    b_qv = biases[: 2 * dev_width].reshape(2, dev_width)
    b_up = biases[2 * dev_width :]
    out_shard = w_out.T.astype(bf16)
    up_shard = w_up.astype(bf16)
    down_shard = w_down.T.astype(bf16)
    up_out = swap(
        jnp.stack(
            [
                jnp.concatenate([out_shard[:, h * half : (h + 1) * half], up_shard[:, h * unit_width // 2 : (h + 1) * unit_width // 2]], 1)
                for h in range(2)
            ]
        )
    )
    down_halves = swap(
        jnp.stack([down_shard[:, h * unit_width // 2 : (h + 1) * unit_width // 2] for h in range(2)])
    )
    cotangent = swap(cotangent)
    tok_full = jnp.concatenate([tokens, core_exchange(tokens)])
    segments = jnp.where(core == 1, jnp.roll(segments, rows, axis=1), segments)
    qkv_a, qkv_b = gather_pair(qkv_halves[0], qkv_halves[1])
    uo_a, uo_b = gather_pair(up_out[0], up_out[1])
    down_a, down_b = gather_pair(down_halves[0], down_halves[1])
    qkv16 = jnp.stack(
        [jnp.concatenate([part[:, k * half : (k + 1) * half] for part in (qkv_a, qkv_b)], 1) for k in range(3)]
    )
    out_t = jnp.concatenate([uo_a[:, :half], uo_b[:, :half]], 1)
    up16 = jnp.concatenate([uo_a[:, half:], uo_b[:, half:]], 1)
    down_t = jnp.concatenate([down_a, down_b], 1)

    bias_rows = jnp.stack([b_qv[0], jnp.zeros_like(b_qv[0]), b_qv[1]])[:, None, :]
    packed = (
        jnp.einsum("nd,kde->kne", tok_full, qkv16, preferred_element_type=f32) + bias_rows
    ).astype(bf16)
    seg_col = segments.reshape(-1, 1)
    pairs = dev_width // 128
    context, logsum = attend_forward(packed, seg_col, 0, pairs)

    def summed(left, right, form):
        away = jnp.einsum(form, left[rows:], right, preferred_element_type=f32)
        other = core_exchange(away.astype(bf16))
        return jnp.einsum(form, left[:rows], right, preferred_element_type=f32) + other.astype(f32)

    attended = summed(context, out_t, "ne,de->nd")
    first_sum = tokens.astype(f32) + attended + w_vec[0]
    hidden, first_pull = jax.vjp(layer_norm, first_sum, w_vec[2], w_vec[3])
    hidden16 = hidden.astype(bf16)
    hidden_full = jnp.concatenate([hidden16, core_exchange(hidden16)])
    upper = jnp.dot(hidden_full, up16, preferred_element_type=f32) + b_up
    active, gelu_pull = jax.vjp(gelu_exact, upper)
    active16 = active.astype(bf16)
    mixed = summed(active16, down_t, "nf,df->nd")
    second_sum = hidden + mixed + w_vec[1]
    normed, second_pull = jax.vjp(layer_norm, second_sum, w_vec[4], w_vec[5])
    layer_out = swap(normed.astype(bf16))
    second_grad, gain2_grad, shift2_grad = second_pull(cotangent.astype(f32))
    second16 = second_grad.astype(bf16)
    mixed_full = jnp.concatenate([second16, core_exchange(second16)])
    active_grad = jnp.einsum("nd,df->nf", mixed_full, down_t, preferred_element_type=f32)
    down_grad = jnp.einsum("nd,nf->df", mixed_full, active16, preferred_element_type=f32).astype(bf16)
    upper_grad = gelu_pull(active_grad)[0]
    upper16 = upper_grad.astype(bf16)
    up_grad = jnp.einsum("nd,nf->df", hidden_full, upper16, preferred_element_type=f32).astype(bf16)
    hidden_grad = second_grad + summed(upper16, up16, "nf,df->nd")
    first_grad, gain1_grad, shift1_grad = first_pull(hidden_grad)
    first16 = first_grad.astype(bf16)
    attended_full = jnp.concatenate([first16, core_exchange(first16)])
    context_grad = jnp.einsum("nd,de->ne", attended_full, out_t, preferred_element_type=f32).astype(bf16)
    out_grad = jnp.einsum("nd,ne->de", attended_full, context, preferred_element_type=f32).astype(bf16)
    packed16, bqv_local = attend_backward(packed, context_grad, context, logsum, seg_col, 0, pairs)
    qkv_grad = jnp.einsum("nd,kne->kde", tok_full, packed16, preferred_element_type=f32).astype(bf16)
    away = jnp.einsum("kne,kde->nd", packed16[:, rows:], qkv16, preferred_element_type=f32)
    other = core_exchange(away.astype(bf16))
    near = jnp.einsum("kne,kde->nd", packed16[:, :rows], qkv16, preferred_element_type=f32)
    grad_tokens = swap((first_grad + near + other.astype(f32)).astype(bf16))

    down_l, down_r = reduce_pair(down_grad[:, : unit_width // 2], down_grad[:, unit_width // 2 :])
    uo_l, uo_r = reduce_pair(
        *(
            jnp.concatenate([out_grad[:, h * half : (h + 1) * half], up_grad[:, h * unit_width // 2 : (h + 1) * unit_width // 2]], 1)
            for h in range(2)
        )
    )
    qkv_l, qkv_r = reduce_pair(
        *(jnp.concatenate([qkv_grad[k, :, h * half : (h + 1) * half] for k in range(3)], 1) for h in range(2))
    )
    qkv_part = jnp.stack(
        [jnp.concatenate([part[:, k * half : (k + 1) * half] for part in (qkv_l, qkv_r)], 1) for k in range(3)]
    )
    out_part = jnp.concatenate([uo_l[:, :half], uo_r[:, :half]], 1).T
    up_part = jnp.concatenate([uo_l[:, half:], uo_r[:, half:]], 1)
    down_part = jnp.concatenate([down_l, down_r], 1).T

    vec_local = jnp.stack(
        [
            jnp.sum(first_grad, axis=0),
            jnp.sum(second_grad, axis=0),
            gain1_grad,
            shift1_grad,
            gain2_grad,
            shift2_grad,
        ]
    )
    vec_local = vec_local + core_exchange(vec_local)
    early = sum_all(jnp.concatenate([vec_local.reshape(-1), jnp.sum(upper_grad, axis=0)]))
    vec_grad = early[: vec_local.size].reshape(vec_local.shape)
    bup_grad = swap(early[vec_local.size :])
    bqv_grad = swap(sum_all(bqv_local))
    base_rate = 1.0 / math.sqrt(SEQ_LEN * lax.axis_size(("chip", "core")))
    slow_rate = MATRIX_RATE * base_rate
    fast_rate = FASTER_RATE * base_rate
    nm_qkv, nw_qkv, na_qkv = advance(w_qkv, m_qkv, a_qkv, qkv_part, slow_rate)
    nm_bqv, nw_bqv, na_bqv = advance(w_bqv, m_bqv, a_bqv, bqv_grad, slow_rate)
    nm_out, nw_out, na_out = advance(w_out, m_out, a_out, out_part, fast_rate)
    nm_up, nw_up, na_up = advance(w_up, m_up, a_up, up_part, slow_rate)
    nm_bup, nw_bup, na_bup = advance(w_bup, m_bup, a_bup, bup_grad, fast_rate)
    nm_down, nw_down, na_down = advance(w_down, m_down, a_down, down_part, slow_rate)
    nm_vec, nw_vec, na_vec = advance(w_vec, m_vec, a_vec, vec_grad, slow_rate)
    return (
        layer_out,
        grad_tokens,
        nm_qkv,
        nw_qkv,
        na_qkv,
        nm_bqv,
        nw_bqv,
        na_bqv,
        nm_out,
        nw_out,
        na_out,
        nm_up,
        nw_up,
        na_up,
        nm_bup,
        nw_bup,
        na_bup,
        nm_down,
        nw_down,
        na_down,
        nm_vec,
        nw_vec,
        na_vec,
    )


def solution(mesh):
    devices = mesh.devices.reshape(-1, 2, 2)
    split_mesh = Mesh(devices, ("chip", "core", "tensor"))
    dp = ("chip", "core")
    row = P(("chip", "core", "tensor"), None)
    deep = P(None, dp, "tensor")
    wide = P("tensor", dp)
    tall = P(dp, "tensor")
    qv = P(None, "tensor")
    unit = P("tensor")
    in_specs = (row, row, P(dp, None)) + (deep,) * 3 + (qv,) * 3 + (wide,) * 3 + (tall,) * 3 + (unit,) * 3 + (wide,) * 3 + (P(),) * 3
    out_specs = (row, row) + in_specs[3:]
    return jax.shard_map(body, mesh=split_mesh, in_specs=in_specs, out_specs=out_specs, check_vma=False)
```

```python
import functools
import math

import jax
import jax.numpy as jnp
from jax import lax
from jax.experimental import pallas as pl
from jax.experimental.pallas import tpu as pltpu
from jax.sharding import Mesh, PartitionSpec as P

HEAD_DIM = 64
SEQ_LEN = 1024


NORM_EPS = 1e-05
MOMENTUM = 0.9
AVERAGE = 0.75
MATRIX_RATE = 0.05
FASTER_RATE = 0.25


def layer_norm(values, gain, shift):
    centred = values - jnp.mean(values, axis=-1, keepdims=True)
    spread = jnp.mean(centred * centred, axis=-1, keepdims=True)
    return centred * lax.rsqrt(spread + NORM_EPS) * gain + shift


def gelu_exact(values):
    return jax.nn.gelu(values, approximate=False)


def advance(weight, moment, average, gradient, step_rate):
    new_moment = MOMENTUM * moment + gradient
    new_weight = weight - step_rate * (gradient + MOMENTUM * new_moment)
    new_average = AVERAGE * average + (1.0 - AVERAGE) * new_weight
    return (new_moment, new_weight, new_average)


NT = (((1,), (1,)), ((), ()))
TN = (((0,), (0,)), ((), ()))
FAR = -1e30


def dot32(left, right, dims=(((1,), (0,)), ((), ()))):
    return lax.dot_general(left, right, dims, preferred_element_type=jnp.float32)


def three_terms(values):
    high = values.astype(jnp.bfloat16).astype(jnp.float32)
    rest = values - high
    middle = rest.astype(jnp.bfloat16).astype(jnp.float32)
    return (high, middle, rest - middle)


def place(lane, terms, other):
    high, middle, low = terms
    return jnp.where(lane == 63, high, jnp.where(lane == 62, middle, jnp.where(lane == 61, low, other)))


def forward_kernel(q_ref, k_ref, v_ref, seg_ref, out_ref, lse_ref, *, block):
    f32, bf16 = jnp.float32, jnp.bfloat16
    rows = q_ref.shape[0]
    lanes = lax.broadcasted_iota(jnp.int32, (rows, 128), 1)
    lower = lanes < HEAD_DIM
    lane = lanes & 63
    same = lane == seg_ref[...]
    q_mark = jnp.where(same, 1.0, 0.0)
    k_mark = jnp.where(same, 0.0, FAR)
    query = q_ref[...].astype(f32)
    keys = k_ref[...].astype(f32) * 0.125
    value = v_ref[...].astype(f32)
    q_heads = [jnp.where(lower, query, q_mark).astype(bf16), jnp.where(lower, q_mark, query).astype(bf16)]
    k_heads = [jnp.where(lower, keys, k_mark).astype(bf16), jnp.where(lower, k_mark, keys).astype(bf16)]
    v_heads = [jnp.where(lower, value, 1.0).astype(bf16), jnp.where(lower, 1.0, value).astype(bf16)]
    low = lower[:block]
    for start in range(0, rows, block):
        parts = []
        for head in range(2):
            scores = dot32(q_heads[head][start : start + block], k_heads[head], NT)
            top = jnp.max(scores, axis=1, keepdims=True)
            weights = jnp.exp(scores - top).astype(bf16)
            parts.append((dot32(weights, v_heads[head]), top))
        (first, top0), (second, top1) = parts
        total = pltpu.roll(jnp.where(low, second, first), HEAD_DIM, 1)
        out_ref[start : start + block, :] = (jnp.where(low, first, second) / total).astype(bf16)
        lse_ref[start : start + block, :] = jnp.where(low, top0, top1) + jnp.log(total)


def backward_kernel(q_ref, k_ref, v_ref, g_ref, o_ref, lse_ref, seg_ref, d_ref, sum_ref, *, block):
    f32, bf16 = jnp.float32, jnp.bfloat16
    rows = q_ref.shape[0]
    lanes = lax.broadcasted_iota(jnp.int32, (rows, 128), 1)
    lower = lanes < HEAD_DIM
    lane = lanes & 63
    same = lane == seg_ref[...]
    query = q_ref[...].astype(f32)
    keys = k_ref[...].astype(f32) * 0.125
    value = v_ref[...].astype(f32)
    grad = g_ref[...].astype(f32)
    lse = pltpu.roll(lse_ref[...], HEAD_DIM, 1)
    q_mark = place(lane, three_terms(-lse), jnp.where(same, 1.0, 0.0))
    k_mark = jnp.where(lane > 60, 1.0, jnp.where(same, 0.0, FAR))
    inner = grad * o_ref[...].astype(f32)
    inner0 = jnp.sum(jnp.where(lower, inner, 0.0), axis=1, keepdims=True)
    inner1 = jnp.sum(jnp.where(lower, 0.0, inner), axis=1, keepdims=True)
    g_mark = place(lane, three_terms(-jnp.where(lower, inner1, inner0)), 0.0)
    v_mark = jnp.where(lane > 60, 1.0, 0.0)

    def heads(values, mark):
        return [jnp.where(lower, values, mark).astype(bf16), jnp.where(lower, mark, values).astype(bf16)]

    q_heads, k_heads = heads(query, q_mark), heads(keys, k_mark)
    v_heads, g_heads = heads(value, v_mark), heads(grad, g_mark)
    q_small = (query * 0.125).astype(bf16)
    k_small = keys.astype(bf16)
    grad16 = g_ref[...]
    low = lower[:block]
    q_grads = [None, None]
    spot = pl.program_id(0) * 128
    places = [pl.ds(pl.multiple_of(k * (d_ref.shape[1] // 3) + spot, 128), 128) for k in range(3)]
    v_sum = jnp.zeros((1, 128), f32)
    for start in range(0, rows, block):
        stop = start + block
        dv, dk = [], []
        for head in range(2):
            probs = jnp.exp(dot32(k_heads[head][start:stop], q_heads[head], NT))
            delta = dot32(v_heads[head][start:stop], g_heads[head], NT)
            dv.append(dot32(probs.astype(bf16), grad16))
            change = (probs * delta).astype(bf16)
            dk.append(dot32(change, q_small))
            part = dot32(change, k_small[start:stop], TN)
            q_grads[head] = part if q_grads[head] is None else q_grads[head] + part
        v_grad = jnp.where(low, dv[0], dv[1])
        v_sum = v_sum + jnp.sum(v_grad, axis=0, keepdims=True)
        d_ref[start:stop, places[1]] = jnp.where(low, dk[0], dk[1]).astype(bf16)
        d_ref[start:stop, places[2]] = v_grad.astype(bf16)
    q_grad = jnp.where(lower, q_grads[0], q_grads[1])
    d_ref[:, places[0]] = q_grad.astype(bf16)
    sum_ref[0:1, :] = jnp.sum(q_grad, axis=0, keepdims=True)
    sum_ref[1:2, :] = v_sum


def part_specs(rows, pairs):
    return [pl.BlockSpec((rows, 128), lambda i, k=k: (0, k * pairs + i)) for k in range(3)]


def attend_forward(packed, seg_col, block=512):
    rows, width = packed.shape
    pairs = width // 384
    flat = pl.BlockSpec((rows, 128), lambda i: (0, i))
    return pl.pallas_call(
        functools.partial(forward_kernel, block=block),
        grid=(pairs,),
        in_specs=part_specs(rows, pairs) + [pl.BlockSpec((rows, 1), lambda i: (0, 0))],
        out_specs=[flat, flat],
        out_shape=[
            jax.ShapeDtypeStruct((rows, pairs * 128), jnp.bfloat16),
            jax.ShapeDtypeStruct((rows, pairs * 128), jnp.float32),
        ],
        compiler_params=pltpu.CompilerParams(vmem_limit_bytes=48 * 2**20),
        name="attend_forward",
    )(packed, packed, packed, seg_col)


def attend_backward(packed, grad, context, lse, seg_col, block=256):
    rows, width = packed.shape
    pairs = width // 384
    flat = pl.BlockSpec((rows, 128), lambda i: (0, i))
    return pl.pallas_call(
        functools.partial(backward_kernel, block=block),
        grid=(pairs,),
        in_specs=part_specs(rows, pairs) + [flat] * 3 + [pl.BlockSpec((rows, 1), lambda i: (0, 0))],
        out_specs=[
            pl.BlockSpec((rows, width), lambda i: (0, 0)),
            pl.BlockSpec((2, 128), lambda i: (0, i)),
        ],
        out_shape=[
            jax.ShapeDtypeStruct((rows, width), jnp.bfloat16),
            jax.ShapeDtypeStruct((2, pairs * 128), jnp.float32),
        ],
        compiler_params=pltpu.CompilerParams(vmem_limit_bytes=48 * 2**20),
        name="attend_backward",
    )(packed, packed, packed, grad, context, lse, seg_col)


SWAP = [(core * 2 + side, side * 2 + core) for core in range(2) for side in range(2)]
FLIP = [(0, 1), (1, 0)]


def swap(values):
    return lax.ppermute(values, ("core", "tensor"), SWAP)


def core_exchange(values):
    return lax.ppermute(values, "core", FLIP)


def y_exchange(values):
    return lax.ppermute(values, "tensor", FLIP)


def chip_exchange(values, mask):
    count = lax.axis_size("chip")
    return lax.ppermute(values, "chip", [(k, k ^ mask) for k in range(count)])


def bits():
    chip = lax.axis_index("chip")
    return (lax.axis_index("tensor"), chip & 1, (chip >> 1) & 1, (chip >> 2) & 1)


STAGES = (
    y_exchange,
    lambda values: chip_exchange(values, 1),
    lambda values: chip_exchange(values, 2),
    lambda values: chip_exchange(values, 4),
)
Y, X, Z1, Z2 = range(4)


def tie(*values):
    return lax.optimization_barrier(values)


def join(mine, other, stage, axis):
    first = bits()[stage] == 0
    return jnp.where(first, jnp.stack([mine, other], axis), jnp.stack([other, mine], axis))


class Gather:
    def __init__(self, both):
        self.rows, self.width = both.shape[1:]
        self.native = lax.axis_size("chip") != 8
        self.flight = ()
        self.held = (both,)
        self.step = 0

    def start(self):
        if self.native:
            return
        if self.step == 0:
            self.flight = (STAGES[Z2](self.held[0]),)
        elif self.step == 1:
            self.flight = (STAGES[Z1](self.held[0]),)
        elif self.step == 2:
            self.flight = (STAGES[X](self.held[0]), STAGES[Y](self.held[1]))
        else:
            self.flight = (STAGES[Y](self.held[0]), STAGES[X](self.held[1]))

    def finish(self):
        if self.native:
            return
        if self.step == 0:
            self.held = (join(self.held[0], self.flight[0], Z2, 1),)
        elif self.step == 1:
            both = join(self.held[0], self.flight[0], Z1, 2)
            self.held = (both[0], both[1])
        elif self.step == 2:
            left, right = self.held
            self.held = (join(left, self.flight[0], X, 2), join(right, self.flight[1], Y, 2))
        else:
            left, right = self.held
            self.held = (join(left, self.flight[0], Y, 3), join(right, self.flight[1], X, 2))
        self.flight = ()
        self.step += 1

    def result(self):
        if self.native:
            return tuple(lax.all_gather(self.held[0][k], ("chip", "tensor"), axis=0, tiled=True) for k in range(2))
        return tuple(part.reshape(16 * self.rows, self.width) for part in self.held)


class Reduce:
    def __init__(self, left, right):
        self.width = left.shape[1]
        self.native = lax.axis_size("chip") != 8
        self.held, self.flight = (left, right), ()
        self.step = 0
        if not self.native:
            self.held = tuple(part.reshape(2, 2, 2, 2, -1, self.width) for part in self.held)

    def start(self):
        if self.native:
            return
        if self.step == 0:
            plan = ((Y, 3), (X, 2))
        elif self.step == 1:
            plan = ((X, 2), (Y, 2))
        elif self.step == 2:
            plan = ((Z1, 2),)
        else:
            plan = ((Z2, 1),)
        self.keep, self.flight = [], []
        for part, (stage, axis) in zip(self.held, plan):
            bit = bits()[stage]
            self.keep.append(lax.dynamic_index_in_dim(part, bit, axis, keepdims=False))
            self.flight.append(STAGES[stage](lax.dynamic_index_in_dim(part, 1 - bit, axis, keepdims=False)))
        self.flight = tuple(self.flight)

    def finish(self):
        if self.native:
            return
        total = tuple(
            (mine.astype(jnp.float32) + other.astype(jnp.float32)).astype(jnp.bfloat16)
            for mine, other in zip(self.keep, self.flight)
        )
        self.held = (jnp.stack(total),) if self.step == 1 else total
        self.flight = ()
        self.step += 1

    def result(self):
        if self.native:
            both = jnp.stack(
                [lax.psum_scatter(p, ("chip", "tensor"), scatter_dimension=0, tiled=True) for p in self.held]
            )
        else:
            both = self.held[0]
        return swap(both)


def arrive(stream, *values):
    count = len(stream.flight)
    out = tie(*stream.flight, *values) if count + len(values) else ()
    stream.flight = out[:count]
    stream.finish()
    return out[count:]


def follow(stream, *values):
    out = tie(*stream.held, *values)
    count = len(stream.held)
    stream.held = out[:count]
    return out[count:]


def sum_all(values):
    if lax.axis_size("chip") != 8:
        return lax.psum(values, ("chip", "tensor"))
    for stage in (Y, X, Z1, Z2):
        values = values + STAGES[stage](values)
    return values


def halves(values, width):
    return (values[:, :width], values[:, width:])


def body(
    tokens,
    cotangent,
    segment_ids,
    w_qkv,
    m_qkv,
    a_qkv,
    w_bqv,
    m_bqv,
    a_bqv,
    w_out,
    m_out,
    a_out,
    w_up,
    m_up,
    a_up,
    w_bup,
    m_bup,
    a_bup,
    w_down,
    m_down,
    a_down,
    w_vec,
    m_vec,
    a_vec,
):
    f32, bf16 = jnp.float32, jnp.bfloat16
    core = lax.axis_index("core")
    dev_width = w_bqv.shape[1]
    unit_width = w_bup.shape[0]
    rows = tokens.shape[0]
    half = dev_width // 2
    unit_half = unit_width // 2
    sides = range(2)

    def full(values):
        return jnp.concatenate([values, core_exchange(values)])

    qkv_shard = w_qkv.astype(bf16)
    qkv_both = swap(
        jnp.stack([jnp.concatenate([qkv_shard[k, :, h * half : (h + 1) * half] for k in range(3)], 1) for h in sides])
    )
    tokens, qkv_order = tie(tokens, qkv_both)
    tokens = swap(tokens)
    out_shard, up_shard, down_shard = w_out.T.astype(bf16), w_up.astype(bf16), w_down.T.astype(bf16)
    rest = jnp.stack(
        [
            jnp.concatenate(
                [
                    out_shard[:, h * half : (h + 1) * half],
                    up_shard[:, h * unit_half : (h + 1) * unit_half],
                    down_shard[:, h * unit_half : (h + 1) * unit_half],
                ],
                1,
            )
            for h in sides
        ]
    )
    small = jnp.concatenate([w_bqv.reshape(-1), w_bup, segment_ids.reshape(-1).astype(f32)])

    qkv = Gather(qkv_order)
    qkv.start()
    tokens, rest, small = arrive(qkv, tokens, rest, small)
    qkv.start()
    rest, small = swap(rest), swap(small)
    tok_full = full(tokens)
    (rest, small, tok_full) = arrive(qkv, rest, small, tok_full)
    qkv.start()
    b_qv = small[: 2 * dev_width].reshape(2, dev_width)
    b_up = small[2 * dev_width : 2 * dev_width + unit_width]
    segments = small[2 * dev_width + unit_width :].astype(jnp.int32).reshape(1, -1)
    segments = jnp.where(core == 1, jnp.roll(segments, rows, axis=1), segments)
    seg_col = segments.reshape(-1, 1)
    upo = Gather(rest[:, :, : half + unit_half])
    down = Gather(rest[:, :, half + unit_half :])
    upo.start()
    arrive(qkv)
    qkv.start()
    (tok_full,) = arrive(upo, tok_full)
    upo.start()
    (tok_full,) = arrive(qkv, tok_full)
    (tok_full,) = arrive(upo, tok_full)
    upo.start()
    down.start()
    qkv_w = qkv.result()

    packed, context, logsum = [], [], []
    for h in sides:
        bias = jnp.concatenate(
            [b_qv[0, h * half : (h + 1) * half], jnp.zeros((half,), f32), b_qv[1, h * half : (h + 1) * half]]
        )
        packed.append((jnp.dot(tok_full, qkv_w[h], preferred_element_type=f32) + bias).astype(bf16))
    for h in sides:
        ctx, lse = attend_forward(packed[h], seg_col)
        context.append(ctx)
        logsum.append(lse)
        if h == 0:
            (packed[1],) = arrive(upo, packed[1])
            upo.start()
            (packed[1],) = arrive(down, packed[1])
            down.start()
    (context[1],) = arrive(upo, context[1])
    uo_w = upo.result()
    out_w = [part[:, :half] for part in uo_w]
    up_w = [part[:, half:] for part in uo_w]
    (context[1],) = arrive(down, context[1])
    down.start()
    cotangent, _ = tie(cotangent, context[1])

    def pair_dot(lefts, rights, form):
        return sum(jnp.einsum(form, left, right, preferred_element_type=f32) for left, right in zip(lefts, rights))

    def summed(lefts, rights, form):
        away = pair_dot([left[rows:] for left in lefts], rights, form)
        other = core_exchange(away.astype(bf16))
        return pair_dot([left[:rows] for left in lefts], rights, form) + other.astype(f32)

    attended = summed(context, out_w, "ne,de->nd")
    first_sum = tokens.astype(f32) + attended + w_vec[0]
    hidden, first_pull = jax.vjp(layer_norm, first_sum, w_vec[2], w_vec[3])
    hidden_full = full(hidden.astype(bf16))
    active16, gelu_pulls = [], []
    for h in sides:
        upper = jnp.dot(hidden_full, up_w[h], preferred_element_type=f32) + b_up[h * unit_half : (h + 1) * unit_half]
        active, pull = jax.vjp(gelu_exact, upper)
        active16.append(active.astype(bf16))
        gelu_pulls.append(pull)
        if h == 0:
            (hidden_full,) = arrive(down, hidden_full)
            down.start()
    (active16[1],) = arrive(down, active16[1])
    down_w = down.result()
    cotangent = swap(cotangent)
    mixed = summed(active16, down_w, "nf,df->nd")
    second_sum = hidden + mixed + w_vec[1]
    normed, second_pull = jax.vjp(layer_norm, second_sum, w_vec[4], w_vec[5])
    layer_out = normed.astype(bf16)
    second_grad, gain2_grad, shift2_grad = second_pull(cotangent.astype(f32))
    second_full = full(second_grad.astype(bf16))
    down_grads = [jnp.einsum("nd,nf->df", second_full, active16[h], preferred_element_type=f32).astype(bf16) for h in sides]
    (second_full, *down_grads) = tie(second_full, *down_grads)
    down_sum = Reduce(*down_grads)
    down_sum.start()
    upper_grads, upper16, up_grads = [], [], []
    for h in sides:
        active_grad = jnp.einsum("nd,df->nf", second_full, down_w[h], preferred_element_type=f32)
        upper_grads.append(gelu_pulls[h](active_grad)[0])
        upper16.append(upper_grads[h].astype(bf16))
    for h in sides:
        up_grads.append(jnp.einsum("nd,nf->df", hidden_full, upper16[h], preferred_element_type=f32).astype(bf16))
    (upper16[0], upper16[1], *up_grads) = arrive(down_sum, *upper16, *up_grads)
    down_sum.start()
    hidden_grad = second_grad + summed(upper16, up_w, "nf,df->nd")
    first_grad, gain1_grad, shift1_grad = first_pull(hidden_grad)
    first_full = full(first_grad.astype(bf16))
    out_grads = [jnp.einsum("nd,ne->de", first_full, context[h], preferred_element_type=f32).astype(bf16) for h in sides]
    (first_full, *out_grads) = arrive(down_sum, first_full, *out_grads)
    upo_sum = Reduce(*(jnp.concatenate([out_grads[h], up_grads[h]], 1) for h in sides))
    (first_full,) = follow(upo_sum, first_full)
    upo_sum.start()
    down_sum.start()
    context_grads = [
        jnp.einsum("nd,de->ne", first_full, out_w[h], preferred_element_type=f32).astype(bf16) for h in sides
    ]
    vec_local = jnp.stack(
        [
            jnp.sum(first_grad, axis=0),
            jnp.sum(second_grad, axis=0),
            gain1_grad,
            shift1_grad,
            gain2_grad,
            shift2_grad,
        ]
    )
    bup_local = jnp.concatenate([jnp.sum(part, axis=0) for part in upper_grads])
    packed16, bias_sums = [None, None], [None, None]
    packed16[0], bias_sums[0] = attend_backward(packed[0], context_grads[0], context[0], logsum[0], seg_col)
    (context_grads[1], packed16[0], vec_local, layer_out) = arrive(
        down_sum, context_grads[1], packed16[0], vec_local, layer_out
    )
    down_sum.start()
    vec_local = vec_local + core_exchange(vec_local)
    early = sum_all(jnp.concatenate([vec_local.reshape(-1), bup_local]))
    vec_grad = early[: vec_local.size].reshape(vec_local.shape)
    packed16[1], bias_sums[1] = attend_backward(packed[1], context_grads[1], context[1], logsum[1], seg_col)
    (packed16[1],) = arrive(upo_sum, packed16[1])
    upo_sum.start()
    (packed16[1], vec_grad) = arrive(down_sum, packed16[1], vec_grad)

    qkv_grads = [
        jnp.dot(tok_full.T, packed16[h], preferred_element_type=f32).astype(bf16) for h in sides
    ]
    layer_out, vec_grad, *qkv_grads = arrive(upo_sum, layer_out, vec_grad, *qkv_grads)
    qkv_sum = Reduce(*qkv_grads)
    qkv_sum.start()
    upo_sum.start()
    bup_grad = early[vec_local.size :]
    away = pair_dot([part[rows:] for part in packed16], qkv_w, "ne,de->nd")
    other = core_exchange(away.astype(bf16))
    near = pair_dot([part[:rows] for part in packed16], qkv_w, "ne,de->nd")
    grad_tokens = (first_grad + near + other.astype(f32)).astype(bf16)
    bqv_local = jnp.concatenate(bias_sums, 1)
    (grad_tokens,) = arrive(upo_sum, grad_tokens)
    upo_sum.start()
    (grad_tokens, bqv_local, bup_grad, layer_out) = arrive(qkv_sum, grad_tokens, bqv_local, bup_grad, layer_out)
    qkv_sum.start()
    layer_out = swap(layer_out)
    bqv_grad = sum_all(bqv_local)
    down_both = down_sum.result()
    (grad_tokens, bqv_grad) = arrive(upo_sum, grad_tokens, bqv_grad)
    arrive(qkv_sum)
    qkv_sum.start()
    grad_tokens = swap(grad_tokens)
    upo_both = upo_sum.result()
    arrive(qkv_sum)
    qkv_sum.start()
    tail = swap(jnp.concatenate([bqv_grad.reshape(-1), bup_grad]))
    bqv_grad = tail[: bqv_grad.size].reshape(bqv_grad.shape)
    bup_grad = tail[bqv_grad.size :]
    arrive(qkv_sum)
    qkv_both = qkv_sum.result().astype(f32)
    upo_both, down_both = upo_both.astype(f32), down_both.astype(f32)
    qkv_part = jnp.stack(
        [jnp.concatenate([qkv_both[h, :, k * half : (k + 1) * half] for h in sides], 1) for k in range(3)]
    )
    out_part = jnp.concatenate([upo_both[h, :, :half] for h in sides], 1).T
    up_part = jnp.concatenate([upo_both[h, :, half:] for h in sides], 1)
    down_part = jnp.concatenate([down_both[h] for h in sides], 1).T
    base_rate = 1.0 / math.sqrt(SEQ_LEN * lax.axis_size(("chip", "core")))
    slow_rate = MATRIX_RATE * base_rate
    fast_rate = FASTER_RATE * base_rate
    nm_qkv, nw_qkv, na_qkv = advance(w_qkv, m_qkv, a_qkv, qkv_part, slow_rate)
    nm_bqv, nw_bqv, na_bqv = advance(w_bqv, m_bqv, a_bqv, bqv_grad, slow_rate)
    nm_out, nw_out, na_out = advance(w_out, m_out, a_out, out_part, fast_rate)
    nm_up, nw_up, na_up = advance(w_up, m_up, a_up, up_part, slow_rate)
    nm_bup, nw_bup, na_bup = advance(w_bup, m_bup, a_bup, bup_grad, fast_rate)
    nm_down, nw_down, na_down = advance(w_down, m_down, a_down, down_part, slow_rate)
    nm_vec, nw_vec, na_vec = advance(w_vec, m_vec, a_vec, vec_grad, slow_rate)
    return (
        layer_out,
        grad_tokens,
        nm_qkv,
        nw_qkv,
        na_qkv,
        nm_bqv,
        nw_bqv,
        na_bqv,
        nm_out,
        nw_out,
        na_out,
        nm_up,
        nw_up,
        na_up,
        nm_bup,
        nw_bup,
        na_bup,
        nm_down,
        nw_down,
        na_down,
        nm_vec,
        nw_vec,
        na_vec,
    )


def solution(mesh):
    devices = mesh.devices.reshape(-1, 2, 2)
    split_mesh = Mesh(devices, ("chip", "core", "tensor"))
    dp = ("chip", "core")
    row = P(("chip", "core", "tensor"), None)
    deep = P(None, dp, "tensor")
    wide = P("tensor", dp)
    tall = P(dp, "tensor")
    qv = P(None, "tensor")
    unit = P("tensor")
    in_specs = (row, row, P(dp, None)) + (deep,) * 3 + (qv,) * 3 + (wide,) * 3 + (tall,) * 3 + (unit,) * 3 + (wide,) * 3 + (P(),) * 3
    out_specs = (row, row) + in_specs[3:]
    return jax.shard_map(body, mesh=split_mesh, in_specs=in_specs, out_specs=out_specs, check_vma=False)
```

```python
import functools
import math

import jax
import jax.numpy as jnp
from jax import lax
from jax.experimental import pallas as pl
from jax.experimental.pallas import tpu as pltpu
from jax.sharding import Mesh, PartitionSpec as P

HEAD_DIM = 64
SEQ_LEN = 1024


NORM_EPS = 1e-05
MOMENTUM = 0.9
AVERAGE = 0.75
MATRIX_RATE = 0.05
FASTER_RATE = 0.25


def layer_norm(values, gain, shift):
    centred = values - jnp.mean(values, axis=-1, keepdims=True)
    spread = jnp.mean(centred * centred, axis=-1, keepdims=True)
    return centred * lax.rsqrt(spread + NORM_EPS) * gain + shift


def gelu_exact(values):
    return jax.nn.gelu(values, approximate=False)


def advance(weight, moment, average, gradient, step_rate):
    new_moment = MOMENTUM * moment + gradient
    new_weight = weight - step_rate * (gradient + MOMENTUM * new_moment)
    new_average = AVERAGE * average + (1.0 - AVERAGE) * new_weight
    return (new_moment, new_weight, new_average)


NT = (((1,), (1,)), ((), ()))
TN = (((0,), (0,)), ((), ()))
FAR = -1e30


def dot32(left, right, dims=(((1,), (0,)), ((), ()))):
    return lax.dot_general(left, right, dims, preferred_element_type=jnp.float32)


def three_terms(values):
    high = values.astype(jnp.bfloat16).astype(jnp.float32)
    rest = values - high
    middle = rest.astype(jnp.bfloat16).astype(jnp.float32)
    return (high, middle, rest - middle)


def place(lane, terms, other):
    high, middle, low = terms
    return jnp.where(lane == 63, high, jnp.where(lane == 62, middle, jnp.where(lane == 61, low, other)))


def forward_kernel(q_ref, k_ref, v_ref, seg_ref, out_ref, lse_ref, *, block):
    f32, bf16 = jnp.float32, jnp.bfloat16
    rows = q_ref.shape[0]
    lanes = lax.broadcasted_iota(jnp.int32, (rows, 128), 1)
    lower = lanes < HEAD_DIM
    lane = lanes & 63
    same = lane == seg_ref[...]
    q_mark = jnp.where(same, 1.0, 0.0)
    k_mark = jnp.where(same, 0.0, FAR)
    query = q_ref[...].astype(f32)
    keys = k_ref[...].astype(f32) * 0.125
    value = v_ref[...].astype(f32)
    q_heads = [jnp.where(lower, query, q_mark).astype(bf16), jnp.where(lower, q_mark, query).astype(bf16)]
    k_heads = [jnp.where(lower, keys, k_mark).astype(bf16), jnp.where(lower, k_mark, keys).astype(bf16)]
    v_heads = [jnp.where(lower, value, 1.0).astype(bf16), jnp.where(lower, 1.0, value).astype(bf16)]
    low = lower[:block]
    for start in range(0, rows, block):
        parts = []
        for head in range(2):
            scores = dot32(q_heads[head][start : start + block], k_heads[head], NT)
            top = jnp.max(scores, axis=1, keepdims=True)
            weights = jnp.exp(scores - top).astype(bf16)
            parts.append((dot32(weights, v_heads[head]), top))
        (first, top0), (second, top1) = parts
        total = pltpu.roll(jnp.where(low, second, first), HEAD_DIM, 1)
        out_ref[start : start + block, :] = (jnp.where(low, first, second) / total).astype(bf16)
        lse_ref[start : start + block, :] = jnp.where(low, top0, top1) + jnp.log(total)


def backward_kernel(q_ref, k_ref, v_ref, g_ref, o_ref, lse_ref, seg_ref, d_ref, sum_ref, *, block):
    f32, bf16 = jnp.float32, jnp.bfloat16
    rows = q_ref.shape[0]
    lanes = lax.broadcasted_iota(jnp.int32, (rows, 128), 1)
    lower = lanes < HEAD_DIM
    lane = lanes & 63
    same = lane == seg_ref[...]
    query = q_ref[...].astype(f32)
    keys = k_ref[...].astype(f32) * 0.125
    value = v_ref[...].astype(f32)
    grad = g_ref[...].astype(f32)
    lse = pltpu.roll(lse_ref[...], HEAD_DIM, 1)
    q_mark = place(lane, three_terms(-lse), jnp.where(same, 1.0, 0.0))
    k_mark = jnp.where(lane > 60, 1.0, jnp.where(same, 0.0, FAR))
    inner = grad * o_ref[...].astype(f32)
    inner0 = jnp.sum(jnp.where(lower, inner, 0.0), axis=1, keepdims=True)
    inner1 = jnp.sum(jnp.where(lower, 0.0, inner), axis=1, keepdims=True)
    g_mark = place(lane, three_terms(-jnp.where(lower, inner1, inner0)), 0.0)
    v_mark = jnp.where(lane > 60, 1.0, 0.0)

    def heads(values, mark):
        return [jnp.where(lower, values, mark).astype(bf16), jnp.where(lower, mark, values).astype(bf16)]

    q_heads, k_heads = heads(query, q_mark), heads(keys, k_mark)
    v_heads, g_heads = heads(value, v_mark), heads(grad, g_mark)
    q_small = (query * 0.125).astype(bf16)
    k_small = keys.astype(bf16)
    grad16 = g_ref[...]
    low = lower[:block]
    q_grads = [None, None]
    spot = pl.program_id(0) * 128
    places = [pl.ds(pl.multiple_of(k * (d_ref.shape[1] // 3) + spot, 128), 128) for k in range(3)]
    v_sum = jnp.zeros((1, 128), f32)
    for start in range(0, rows, block):
        stop = start + block
        dv, dk = [], []
        for head in range(2):
            probs = jnp.exp(dot32(k_heads[head][start:stop], q_heads[head], NT))
            delta = dot32(v_heads[head][start:stop], g_heads[head], NT)
            dv.append(dot32(probs.astype(bf16), grad16))
            change = (probs * delta).astype(bf16)
            dk.append(dot32(change, q_small))
            part = dot32(change, k_small[start:stop], TN)
            q_grads[head] = part if q_grads[head] is None else q_grads[head] + part
        v_grad = jnp.where(low, dv[0], dv[1])
        v_sum = v_sum + jnp.sum(v_grad, axis=0, keepdims=True)
        d_ref[start:stop, places[1]] = jnp.where(low, dk[0], dk[1]).astype(bf16)
        d_ref[start:stop, places[2]] = v_grad.astype(bf16)
    q_grad = jnp.where(lower, q_grads[0], q_grads[1])
    d_ref[:, places[0]] = q_grad.astype(bf16)
    sum_ref[0:1, :] = jnp.sum(q_grad, axis=0, keepdims=True)
    sum_ref[1:2, :] = v_sum


def part_specs(rows, pairs):
    return [pl.BlockSpec((rows, 128), lambda i, k=k: (0, k * pairs + i)) for k in range(3)]


def attend_forward(packed, seg_col, block=512):
    rows, width = packed.shape
    pairs = width // 384
    flat = pl.BlockSpec((rows, 128), lambda i: (0, i))
    return pl.pallas_call(
        functools.partial(forward_kernel, block=block),
        grid=(pairs,),
        in_specs=part_specs(rows, pairs) + [pl.BlockSpec((rows, 1), lambda i: (0, 0))],
        out_specs=[flat, flat],
        out_shape=[
            jax.ShapeDtypeStruct((rows, pairs * 128), jnp.bfloat16),
            jax.ShapeDtypeStruct((rows, pairs * 128), jnp.float32),
        ],
        compiler_params=pltpu.CompilerParams(vmem_limit_bytes=48 * 2**20),
        name="attend_forward",
    )(packed, packed, packed, seg_col)


def attend_backward(packed, grad, context, lse, seg_col, block=256):
    rows, width = packed.shape
    pairs = width // 384
    flat = pl.BlockSpec((rows, 128), lambda i: (0, i))
    return pl.pallas_call(
        functools.partial(backward_kernel, block=block),
        grid=(pairs,),
        in_specs=part_specs(rows, pairs) + [flat] * 3 + [pl.BlockSpec((rows, 1), lambda i: (0, 0))],
        out_specs=[
            pl.BlockSpec((rows, width), lambda i: (0, 0)),
            pl.BlockSpec((2, 128), lambda i: (0, i)),
        ],
        out_shape=[
            jax.ShapeDtypeStruct((rows, width), jnp.bfloat16),
            jax.ShapeDtypeStruct((2, pairs * 128), jnp.float32),
        ],
        compiler_params=pltpu.CompilerParams(vmem_limit_bytes=48 * 2**20),
        name="attend_backward",
    )(packed, packed, packed, grad, context, lse, seg_col)


CROSS = [(1, 2), (2, 1)]
FLIP = [(0, 1), (1, 0)]


def cross(values):
    return lax.ppermute(values, ("core", "tensor"), CROSS)


def settle(mine, other):
    return jnp.where(lax.axis_index("core") == lax.axis_index("tensor"), mine, other)


def core_exchange(values):
    return lax.ppermute(values, "core", FLIP)


def y_exchange(values):
    return lax.ppermute(values, "tensor", FLIP)


def chip_exchange(values, mask):
    count = lax.axis_size("chip")
    return lax.ppermute(values, "chip", [(k, k ^ mask) for k in range(count)])


def bits():
    chip = lax.axis_index("chip")
    return (lax.axis_index("tensor"), chip & 1, (chip >> 1) & 1, (chip >> 2) & 1)


STAGES = (
    y_exchange,
    lambda values: chip_exchange(values, 1),
    lambda values: chip_exchange(values, 2),
    lambda values: chip_exchange(values, 4),
)
Y, X, Z1, Z2 = range(4)


def join(mine, other, stage, axis):
    first = bits()[stage] == 0
    return jnp.where(first, jnp.stack([mine, other], axis), jnp.stack([other, mine], axis))


class Gather:
    def __init__(self, held, step=0):
        self.rows, self.width = held[0].shape[-2:]
        self.native = lax.axis_size("chip") != 8
        self.flight = ()
        self.held = held
        self.step = step

    def fork(self, width):
        return (
            Gather(tuple(part[..., :width] for part in self.held), self.step),
            Gather(tuple(part[..., width:] for part in self.held), self.step),
        )

    def start(self):
        if self.native:
            return
        if self.step == 0:
            self.flight = (STAGES[Z2](self.held[0]),)
        elif self.step == 1:
            self.flight = (STAGES[Z1](self.held[0]),)
        elif self.step == 2:
            self.flight = (STAGES[X](self.held[0]), STAGES[Y](self.held[1]))
        else:
            self.flight = (STAGES[Y](self.held[0]), STAGES[X](self.held[1]))

    def finish(self):
        if self.native:
            return
        if self.step == 0:
            self.held = (join(self.held[0], self.flight[0], Z2, 1),)
        elif self.step == 1:
            both = join(self.held[0], self.flight[0], Z1, 2)
            self.held = (both[0], both[1])
        elif self.step == 2:
            left, right = self.held
            self.held = (join(left, self.flight[0], X, 2), join(right, self.flight[1], Y, 2))
        else:
            left, right = self.held
            self.held = (join(left, self.flight[0], Y, 3), join(right, self.flight[1], X, 2))
        self.flight = ()
        self.step += 1

    def result(self):
        if self.native:
            return tuple(lax.all_gather(self.held[0][k], ("chip", "tensor"), axis=0, tiled=True) for k in range(2))
        return tuple(part.reshape(16 * self.rows, self.width) for part in self.held)


class Reduce:
    def __init__(self, left, right):
        self.width = left.shape[1]
        self.native = lax.axis_size("chip") != 8
        self.held, self.flight = (left, right), ()
        self.step = 0
        if not self.native:
            self.held = tuple(part.reshape(2, 2, 2, 2, -1, self.width) for part in self.held)

    def start(self):
        if self.native:
            return
        if self.step == 0:
            plan = ((Y, 3), (X, 2))
        elif self.step == 1:
            plan = ((X, 2), (Y, 2))
        elif self.step == 2:
            plan = ((Z1, 2),)
        else:
            plan = ((Z2, 1),)
        self.keep, self.flight = [], []
        for part, (stage, axis) in zip(self.held, plan):
            bit = bits()[stage]
            self.keep.append(lax.dynamic_index_in_dim(part, bit, axis, keepdims=False))
            self.flight.append(STAGES[stage](lax.dynamic_index_in_dim(part, 1 - bit, axis, keepdims=False)))
        self.flight = tuple(self.flight)

    def finish(self):
        if self.native:
            return
        total = tuple(
            (mine.astype(jnp.float32) + other.astype(jnp.float32)).astype(jnp.bfloat16)
            for mine, other in zip(self.keep, self.flight)
        )
        self.held = (jnp.stack(total),) if self.step == 1 else total
        self.flight = ()
        self.step += 1

    def result(self):
        if self.native:
            both = jnp.stack(
                [lax.psum_scatter(p, ("chip", "tensor"), scatter_dimension=0, tiled=True) for p in self.held]
            )
        else:
            both = self.held[0]
        return both


class Sum:
    def __init__(self, values):
        self.native = lax.axis_size("chip") != 8
        if self.native:
            values = lax.psum(values, ("chip", "tensor"))
        self.held, self.flight, self.step = (values,), (), 0

    def start(self):
        if not self.native:
            self.flight = (STAGES[(Z2, Z1, X, Y)[self.step]](self.held[0]),)

    def finish(self):
        if not self.native:
            self.held = (self.held[0] + self.flight[0],)
            self.flight = ()
            self.step += 1


class Order:
    def __init__(self):
        self.now = jnp.zeros((8, 128), jnp.float32)

    def at(self, *values):
        self.now, *values = lax.optimization_barrier((self.now, *values))
        return values

    def arrive(self, stream, *values):
        count = len(stream.flight)
        out = self.at(*stream.flight, *values)
        stream.flight = tuple(out[:count])
        stream.finish()
        return out[count:]


def body(
    tokens,
    cotangent,
    segment_ids,
    w_qkv,
    m_qkv,
    a_qkv,
    w_bqv,
    m_bqv,
    a_bqv,
    w_out,
    m_out,
    a_out,
    w_up,
    m_up,
    a_up,
    w_bup,
    m_bup,
    a_bup,
    w_down,
    m_down,
    a_down,
    w_vec,
    m_vec,
    a_vec,
):
    f32, bf16 = jnp.float32, jnp.bfloat16
    core = lax.axis_index("core")
    dev_width = w_bqv.shape[1]
    unit_width = w_bup.shape[0]
    rows = tokens.shape[0]
    half = dev_width // 2
    unit_half = unit_width // 2
    sides = range(2)
    order = Order()

    def pair_dot(lefts, rights, form):
        return sum(jnp.einsum(form, left, right, preferred_element_type=f32) for left, right in zip(lefts, rights))

    def summed(lefts, rights, form):
        away = pair_dot([left[rows:] for left in lefts], rights, form)
        other = core_exchange(away.astype(bf16))
        return pair_dot([left[:rows] for left in lefts], rights, form) + other.astype(f32)

    def full(values):
        return jnp.concatenate([values, core_exchange(values)])

    qkv_shard = w_qkv.astype(bf16)
    qkv_own = jnp.stack(
        [jnp.concatenate([qkv_shard[k, :, h * half : (h + 1) * half] for k in range(3)], 1) for h in sides]
    )
    qkv_own, tokens, cotangent = order.at(qkv_own, tokens, cotangent)
    qkv_other = cross(qkv_own)
    out_shard, up_shard, down_shard = w_out.T.astype(bf16), w_up.astype(bf16), w_down.T.astype(bf16)
    rest = jnp.stack(
        [
            jnp.concatenate(
                [
                    out_shard[:, h * half : (h + 1) * half],
                    up_shard[:, h * unit_half : (h + 1) * unit_half],
                    down_shard[:, h * unit_half : (h + 1) * unit_half],
                ],
                1,
            )
            for h in sides
        ]
    )
    small = jnp.concatenate([w_bqv.reshape(-1), w_bup, segment_ids.reshape(-1).astype(f32)])
    qkv_other, rest = order.at(qkv_other, rest)
    qkv = Gather((settle(qkv_own, qkv_other),))
    qkv.start()
    rest_other = cross(rest)
    (tokens, small) = order.arrive(qkv, tokens, small)
    qkv.start()
    tok_other = cross(tokens)
    (small,) = order.arrive(qkv, small)
    qkv.start()
    small_other = cross(small)
    (rest_other,) = order.at(rest_other)
    wide = Gather((settle(rest, rest_other),))
    wide.start()
    order.arrive(qkv)
    qkv.start()
    (tok_other,) = order.at(tok_other)
    tokens = settle(tokens, tok_other)
    tok_far = core_exchange(tokens)
    order.arrive(wide)
    wide.start()
    tok_far, small_other = order.at(tok_far, small_other)
    small = settle(small, small_other)
    b_qv = small[: 2 * dev_width].reshape(2, dev_width)
    b_up = small[2 * dev_width : 2 * dev_width + unit_width]
    segments = small[2 * dev_width + unit_width :].astype(jnp.int32).reshape(1, -1)
    segments = jnp.where(core == 1, jnp.roll(segments, rows, axis=1), segments)
    seg_col = segments.reshape(-1, 1)
    tok_full = jnp.concatenate([tokens, tok_far])
    (tok_full, cotangent, seg_col) = order.arrive(qkv, tok_full, cotangent, seg_col)
    cot_other = cross(cotangent)
    qkv_w = qkv.result()

    packed, context, logsum = [], [], []
    for h in sides:
        bias = jnp.concatenate(
            [b_qv[0, h * half : (h + 1) * half], jnp.zeros((half,), f32), b_qv[1, h * half : (h + 1) * half]]
        )
        packed.append((jnp.dot(tok_full, qkv_w[h], preferred_element_type=f32) + bias).astype(bf16))
    for h in sides:
        ctx, lse = attend_forward(packed[h], seg_col)
        context.append(ctx)
        logsum.append(lse)
        if h == 0:
            (context[0], packed[1]) = order.arrive(wide, context[0], packed[1])
            upo, down = wide.fork(half + unit_half)
            upo.start()
    (cot_other, *context) = order.arrive(upo, cot_other, *context)
    upo.start()
    down.start()
    cotangent = settle(cotangent, cot_other)
    context = order.arrive(upo, *context)
    uo_w = upo.result()
    out_w = [part[:, :half] for part in uo_w]
    up_w = [part[:, half:] for part in uo_w]

    attended = summed(context, out_w, "ne,de->nd")
    (attended,) = order.arrive(down, attended)
    down.start()
    first_sum = tokens.astype(f32) + attended + w_vec[0]
    hidden, first_pull = jax.vjp(layer_norm, first_sum, w_vec[2], w_vec[3])
    hidden_full = full(hidden.astype(bf16))
    active16, gelu_pulls = [], []
    for h in sides:
        upper = jnp.dot(hidden_full, up_w[h], preferred_element_type=f32) + b_up[h * unit_half : (h + 1) * unit_half]
        active, pull = jax.vjp(gelu_exact, upper)
        active16.append(active.astype(bf16))
        gelu_pulls.append(pull)
    active16 = order.arrive(down, *active16)
    down_w = down.result()
    mixed = summed(active16, down_w, "nf,df->nd")
    second_sum = hidden + mixed + w_vec[1]
    normed, second_pull = jax.vjp(layer_norm, second_sum, w_vec[4], w_vec[5])
    layer_out = normed.astype(bf16)
    second_grad, gain2_grad, shift2_grad = second_pull(cotangent.astype(f32))
    second_far = core_exchange(second_grad.astype(bf16))
    (second_far, layer_out) = order.at(second_far, layer_out)
    out_other = cross(layer_out)
    second_full = jnp.concatenate([second_grad.astype(bf16), second_far])
    down_grads = [jnp.einsum("nd,nf->df", second_full, active16[h], preferred_element_type=f32).astype(bf16) for h in sides]
    (second_full, *down_grads) = order.at(second_full, *down_grads)
    down_sum = Reduce(*down_grads)
    down_sum.start()
    upper_grads, upper16, up_grads = [], [], []
    for h in sides:
        active_grad = jnp.einsum("nd,df->nf", second_full, down_w[h], preferred_element_type=f32)
        upper_grads.append(gelu_pulls[h](active_grad)[0])
        upper16.append(upper_grads[h].astype(bf16))
    for h in sides:
        up_grads.append(jnp.einsum("nd,nf->df", hidden_full, upper16[h], preferred_element_type=f32).astype(bf16))
    (upper16[0], upper16[1], *up_grads) = order.arrive(down_sum, *upper16, *up_grads)
    down_sum.start()
    hidden_grad = second_grad + summed(upper16, up_w, "nf,df->nd")
    first_grad, gain1_grad, shift1_grad = first_pull(hidden_grad)
    first_full = full(first_grad.astype(bf16))
    out_grads = [jnp.einsum("nd,ne->de", first_full, context[h], preferred_element_type=f32).astype(bf16) for h in sides]
    uo_grads = [jnp.concatenate([out_grads[h], up_grads[h]], 1) for h in sides]
    (first_full, *uo_grads) = order.at(first_full, *uo_grads)
    upo_sum = Reduce(*uo_grads)
    upo_sum.start()
    context_grads = [
        jnp.einsum("nd,de->ne", first_full, out_w[h], preferred_element_type=f32).astype(bf16) for h in sides
    ]
    context_grads = order.arrive(down_sum, *context_grads)
    down_sum.start()
    packed16, bias_sums = [None, None], [None, None]
    packed16[0], bias_sums[0] = attend_backward(packed[0], context_grads[0], context[0], logsum[0], seg_col)
    (out_other, context_grads[1], packed16[0]) = order.arrive(down_sum, out_other, context_grads[1], packed16[0])
    layer_out = settle(layer_out, out_other)
    down_sum.start()
    (context_grads[1], packed16[0]) = order.arrive(upo_sum, context_grads[1], packed16[0])
    upo_sum.start()
    vec_local = jnp.stack(
        [
            jnp.sum(first_grad, axis=0),
            jnp.sum(second_grad, axis=0),
            gain1_grad,
            shift1_grad,
            gain2_grad,
            shift2_grad,
        ]
    )
    bup_local = jnp.concatenate([jnp.sum(part, axis=0) for part in upper_grads])
    vec_far = core_exchange(vec_local)
    packed16[1], bias_sums[1] = attend_backward(packed[1], context_grads[1], context[1], logsum[1], seg_col)
    vec_far, *packed16 = order.at(vec_far, *packed16)
    packed16 = order.arrive(down_sum, *packed16)
    packed16 = order.arrive(upo_sum, *packed16)
    upo_sum.start()
    bqv_local = jnp.concatenate(bias_sums, 1)
    totals = Sum(jnp.concatenate([(vec_local + vec_far).reshape(-1), bqv_local.reshape(-1), bup_local]))
    totals.start()
    down_own = down_sum.result()
    down_other = cross(down_own)

    qkv_grads = [jnp.einsum("nd,ne->de", tok_full, packed16[h], preferred_element_type=f32).astype(bf16) for h in sides]
    (packed16[0], packed16[1], *qkv_grads) = order.arrive(totals, *packed16, *qkv_grads)
    qkv_sum = Reduce(*qkv_grads)
    qkv_sum.start()
    totals.start()
    away = pair_dot([part[rows:] for part in packed16], qkv_w, "ne,de->nd")
    grad_far = core_exchange(away.astype(bf16))
    near = pair_dot([part[:rows] for part in packed16], qkv_w, "ne,de->nd")
    grad_tokens = (first_grad + near + grad_far.astype(f32)).astype(bf16)
    (grad_tokens, down_other) = order.arrive(upo_sum, grad_tokens, down_other)
    upo_sum.start()
    order.arrive(totals)
    totals.start()
    order.arrive(totals)
    (grad_tokens,) = order.arrive(qkv_sum, grad_tokens)
    totals.start()
    qkv_sum.start()
    order.arrive(upo_sum)
    upo_own = upo_sum.result()
    order.arrive(totals)
    vectors = totals.held[0]
    count = vec_local.size
    vec_grad = vectors[:count].reshape(vec_local.shape)
    tail = vectors[count:]
    (upo_own, grad_tokens, tail) = order.arrive(qkv_sum, upo_own, grad_tokens, tail)
    qkv_sum.start()
    tail_other = cross(tail)
    upo_other = cross(upo_own)
    grad_other = cross(grad_tokens)
    order.arrive(qkv_sum)
    qkv_sum.start()
    (tail_other, upo_other, grad_other) = order.at(tail_other, upo_other, grad_other)
    order.arrive(qkv_sum)
    qkv_own = qkv_sum.result()
    qkv_other = cross(qkv_own)
    tail = settle(tail, tail_other)
    bqv_grad = tail[: bqv_local.size].reshape(bqv_local.shape)
    bup_grad = tail[bqv_local.size :]
    grad_tokens = settle(grad_tokens, grad_other)
    upo_both, down_both = settle(upo_own, upo_other).astype(f32), settle(down_own, down_other).astype(f32)
    qkv_both = settle(qkv_own, qkv_other).astype(f32)
    (vec_grad,) = order.at(vec_grad)
    vec_grad = vec_grad + order.now[0, 0]
    qkv_part = jnp.stack(
        [jnp.concatenate([qkv_both[h, :, k * half : (k + 1) * half] for h in sides], 1) for k in range(3)]
    )
    out_part = jnp.concatenate([upo_both[h, :, :half] for h in sides], 1).T
    up_part = jnp.concatenate([upo_both[h, :, half:] for h in sides], 1)
    down_part = jnp.concatenate([down_both[h] for h in sides], 1).T
    base_rate = 1.0 / math.sqrt(SEQ_LEN * lax.axis_size(("chip", "core")))
    slow_rate = MATRIX_RATE * base_rate
    fast_rate = FASTER_RATE * base_rate
    nm_qkv, nw_qkv, na_qkv = advance(w_qkv, m_qkv, a_qkv, qkv_part, slow_rate)
    nm_bqv, nw_bqv, na_bqv = advance(w_bqv, m_bqv, a_bqv, bqv_grad, slow_rate)
    nm_out, nw_out, na_out = advance(w_out, m_out, a_out, out_part, fast_rate)
    nm_up, nw_up, na_up = advance(w_up, m_up, a_up, up_part, slow_rate)
    nm_bup, nw_bup, na_bup = advance(w_bup, m_bup, a_bup, bup_grad, fast_rate)
    nm_down, nw_down, na_down = advance(w_down, m_down, a_down, down_part, slow_rate)
    nm_vec, nw_vec, na_vec = advance(w_vec, m_vec, a_vec, vec_grad, slow_rate)
    return (
        layer_out,
        grad_tokens,
        nm_qkv,
        nw_qkv,
        na_qkv,
        nm_bqv,
        nw_bqv,
        na_bqv,
        nm_out,
        nw_out,
        na_out,
        nm_up,
        nw_up,
        na_up,
        nm_bup,
        nw_bup,
        na_bup,
        nm_down,
        nw_down,
        na_down,
        nm_vec,
        nw_vec,
        na_vec,
    )


def solution(mesh):
    devices = mesh.devices.reshape(-1, 2, 2)
    split_mesh = Mesh(devices, ("chip", "core", "tensor"))
    dp = ("chip", "core")
    row = P(("chip", "core", "tensor"), None)
    deep = P(None, dp, "tensor")
    wide = P("tensor", dp)
    tall = P(dp, "tensor")
    qv = P(None, "tensor")
    unit = P("tensor")
    in_specs = (row, row, P(dp, None)) + (deep,) * 3 + (qv,) * 3 + (wide,) * 3 + (tall,) * 3 + (unit,) * 3 + (wide,) * 3 + (P(),) * 3
    out_specs = (row, row) + in_specs[3:]
    return jax.shard_map(body, mesh=split_mesh, in_specs=in_specs, out_specs=out_specs, check_vma=False)
```

```python
import functools
import math

import jax
import jax.numpy as jnp
from jax import lax
from jax.experimental import pallas as pl
from jax.experimental.pallas import tpu as pltpu
from jax.sharding import Mesh, PartitionSpec as P

HEAD_DIM = 64
SEQ_LEN = 1024


NORM_EPS = 1e-05
MOMENTUM = 0.9
AVERAGE = 0.75
MATRIX_RATE = 0.05
FASTER_RATE = 0.25


def layer_norm(values, gain, shift):
    centred = values - jnp.mean(values, axis=-1, keepdims=True)
    spread = jnp.mean(centred * centred, axis=-1, keepdims=True)
    return centred * lax.rsqrt(spread + NORM_EPS) * gain + shift


def gelu_exact(values):
    return jax.nn.gelu(values, approximate=False)


def advance(weight, moment, average, gradient, step_rate):
    new_moment = MOMENTUM * moment + gradient
    new_weight = weight - step_rate * (gradient + MOMENTUM * new_moment)
    new_average = AVERAGE * average + (1.0 - AVERAGE) * new_weight
    return (new_moment, new_weight, new_average)


NT = (((1,), (1,)), ((), ()))
TN = (((0,), (0,)), ((), ()))
FAR = -1e30


def dot32(left, right, dims=(((1,), (0,)), ((), ()))):
    return lax.dot_general(left, right, dims, preferred_element_type=jnp.float32)


def three_terms(values):
    high = values.astype(jnp.bfloat16).astype(jnp.float32)
    rest = values - high
    middle = rest.astype(jnp.bfloat16).astype(jnp.float32)
    return (high, middle, rest - middle)


def place(lane, terms, other):
    high, middle, low = terms
    return jnp.where(lane == 63, high, jnp.where(lane == 62, middle, jnp.where(lane == 61, low, other)))


def forward_kernel(q_ref, k_ref, v_ref, seg_ref, out_ref, lse_ref, *, block):
    f32, bf16 = jnp.float32, jnp.bfloat16
    rows = q_ref.shape[0]
    lanes = lax.broadcasted_iota(jnp.int32, (rows, 128), 1)
    lower = lanes < HEAD_DIM
    lane = lanes & 63
    same = lane == seg_ref[...]
    q_mark = jnp.where(same, 1.0, 0.0)
    k_mark = jnp.where(same, 0.0, FAR)
    query = q_ref[...].astype(f32)
    keys = k_ref[...].astype(f32) * 0.125
    value = v_ref[...].astype(f32)
    q_heads = [jnp.where(lower, query, q_mark).astype(bf16), jnp.where(lower, q_mark, query).astype(bf16)]
    k_heads = [jnp.where(lower, keys, k_mark).astype(bf16), jnp.where(lower, k_mark, keys).astype(bf16)]
    v_heads = [jnp.where(lower, value, 1.0).astype(bf16), jnp.where(lower, 1.0, value).astype(bf16)]
    low = lower[:block]
    for start in range(0, rows, block):
        parts = []
        for head in range(2):
            scores = dot32(q_heads[head][start : start + block], k_heads[head], NT)
            top = jnp.max(scores, axis=1, keepdims=True)
            weights = jnp.exp(scores - top).astype(bf16)
            parts.append((dot32(weights, v_heads[head]), top))
        (first, top0), (second, top1) = parts
        total = pltpu.roll(jnp.where(low, second, first), HEAD_DIM, 1)
        out_ref[start : start + block, :] = (jnp.where(low, first, second) / total).astype(bf16)
        lse_ref[start : start + block, :] = jnp.where(low, top0, top1) + jnp.log(total)


def backward_kernel(q_ref, k_ref, v_ref, g_ref, o_ref, lse_ref, seg_ref, d_ref, sum_ref, *, block):
    f32, bf16 = jnp.float32, jnp.bfloat16
    rows = q_ref.shape[0]
    lanes = lax.broadcasted_iota(jnp.int32, (rows, 128), 1)
    lower = lanes < HEAD_DIM
    lane = lanes & 63
    same = lane == seg_ref[...]
    query = q_ref[...].astype(f32)
    keys = k_ref[...].astype(f32) * 0.125
    value = v_ref[...].astype(f32)
    grad = g_ref[...].astype(f32)
    lse = pltpu.roll(lse_ref[...], HEAD_DIM, 1)
    q_mark = place(lane, three_terms(-lse), jnp.where(same, 1.0, 0.0))
    k_mark = jnp.where(lane > 60, 1.0, jnp.where(same, 0.0, FAR))
    inner = grad * o_ref[...].astype(f32)
    inner0 = jnp.sum(jnp.where(lower, inner, 0.0), axis=1, keepdims=True)
    inner1 = jnp.sum(jnp.where(lower, 0.0, inner), axis=1, keepdims=True)
    g_mark = place(lane, three_terms(-jnp.where(lower, inner1, inner0)), 0.0)
    v_mark = jnp.where(lane > 60, 1.0, 0.0)

    def heads(values, mark):
        return [jnp.where(lower, values, mark).astype(bf16), jnp.where(lower, mark, values).astype(bf16)]

    q_heads, k_heads = heads(query, q_mark), heads(keys, k_mark)
    v_heads, g_heads = heads(value, v_mark), heads(grad, g_mark)
    q_small = (query * 0.125).astype(bf16)
    k_small = keys.astype(bf16)
    grad16 = g_ref[...]
    low = lower[:block]
    q_grads = [None, None]
    spot = pl.program_id(0) * 128
    places = [pl.ds(pl.multiple_of(k * (d_ref.shape[1] // 3) + spot, 128), 128) for k in range(3)]
    v_sum = jnp.zeros((1, 128), f32)
    for start in range(0, rows, block):
        stop = start + block
        dv, dk = [], []
        for head in range(2):
            probs = jnp.exp(dot32(k_heads[head][start:stop], q_heads[head], NT))
            delta = dot32(v_heads[head][start:stop], g_heads[head], NT)
            dv.append(dot32(probs.astype(bf16), grad16))
            change = (probs * delta).astype(bf16)
            dk.append(dot32(change, q_small))
            part = dot32(change, k_small[start:stop], TN)
            q_grads[head] = part if q_grads[head] is None else q_grads[head] + part
        v_grad = jnp.where(low, dv[0], dv[1])
        v_sum = v_sum + jnp.sum(v_grad, axis=0, keepdims=True)
        d_ref[start:stop, places[1]] = jnp.where(low, dk[0], dk[1]).astype(bf16)
        d_ref[start:stop, places[2]] = v_grad.astype(bf16)
    q_grad = jnp.where(lower, q_grads[0], q_grads[1])
    d_ref[:, places[0]] = q_grad.astype(bf16)
    sum_ref[0:1, :] = jnp.sum(q_grad, axis=0, keepdims=True)
    sum_ref[1:2, :] = v_sum


def part_specs(rows, pairs):
    return [pl.BlockSpec((rows, 128), lambda i, k=k: (0, k * pairs + i)) for k in range(3)]


def attend_forward(packed, seg_col, block=512):
    rows, width = packed.shape
    pairs = width // 384
    flat = pl.BlockSpec((rows, 128), lambda i: (0, i))
    return pl.pallas_call(
        functools.partial(forward_kernel, block=block),
        grid=(pairs,),
        in_specs=part_specs(rows, pairs) + [pl.BlockSpec((rows, 1), lambda i: (0, 0))],
        out_specs=[flat, flat],
        out_shape=[
            jax.ShapeDtypeStruct((rows, pairs * 128), jnp.bfloat16),
            jax.ShapeDtypeStruct((rows, pairs * 128), jnp.float32),
        ],
        compiler_params=pltpu.CompilerParams(vmem_limit_bytes=48 * 2**20),
        name="attend_forward",
    )(packed, packed, packed, seg_col)


def attend_backward(packed, grad, context, lse, seg_col, block=256):
    rows, width = packed.shape
    pairs = width // 384
    flat = pl.BlockSpec((rows, 128), lambda i: (0, i))
    return pl.pallas_call(
        functools.partial(backward_kernel, block=block),
        grid=(pairs,),
        in_specs=part_specs(rows, pairs) + [flat] * 3 + [pl.BlockSpec((rows, 1), lambda i: (0, 0))],
        out_specs=[
            pl.BlockSpec((rows, width), lambda i: (0, 0)),
            pl.BlockSpec((2, 128), lambda i: (0, i)),
        ],
        out_shape=[
            jax.ShapeDtypeStruct((rows, width), jnp.bfloat16),
            jax.ShapeDtypeStruct((2, pairs * 128), jnp.float32),
        ],
        compiler_params=pltpu.CompilerParams(vmem_limit_bytes=48 * 2**20),
        name="attend_backward",
    )(packed, packed, packed, grad, context, lse, seg_col)


CROSS = [(1, 2), (2, 1)]
FLIP = [(0, 1), (1, 0)]


def cross(values):
    return lax.ppermute(values, ("core", "tensor"), CROSS)


def cross_far(values):
    pairs = []
    for chip in range(lax.axis_size("chip")):
        for core in range(2):
            for side in range(2):
                pairs.append((chip * 4 + core * 2 + side, (chip ^ 4) * 4 + side * 2 + core))
    return lax.ppermute(values, ("chip", "core", "tensor"), pairs)


def settle(mine, other):
    return jnp.where(lax.axis_index("core") == lax.axis_index("tensor"), mine, other)


def core_exchange(values):
    return lax.ppermute(values, "core", FLIP)


def y_exchange(values):
    return lax.ppermute(values, "tensor", FLIP)


def chip_exchange(values, mask):
    count = lax.axis_size("chip")
    return lax.ppermute(values, "chip", [(k, k ^ mask) for k in range(count)])


def bits():
    chip = lax.axis_index("chip")
    return (lax.axis_index("tensor"), chip & 1, (chip >> 1) & 1, (chip >> 2) & 1)


STAGES = (
    y_exchange,
    lambda values: chip_exchange(values, 1),
    lambda values: chip_exchange(values, 2),
    lambda values: chip_exchange(values, 4),
)
Y, X, Z1, Z2 = range(4)


def join(mine, other, stage, axis):
    first = bits()[stage] == 0
    return jnp.where(first, jnp.stack([mine, other], axis), jnp.stack([other, mine], axis))


class Gather:
    def __init__(self, held, step=0, mirrored=False):
        self.mirrored = mirrored
        self.rows, self.width = held[0].shape[-2:]
        self.native = lax.axis_size("chip") != 8
        self.flight = ()
        self.held = held
        self.step = step

    def fork(self, width):
        return (
            Gather(tuple(part[..., :width] for part in self.held), self.step),
            Gather(tuple(part[..., width:] for part in self.held), self.step),
        )

    def start(self):
        if self.mirrored:
            far = () if self.native else (cross_far(self.held[0]),)
            self.flight = (cross(self.held[0]),) + far
        elif self.native:
            return
        elif self.step == 0:
            self.flight = (STAGES[Z2](self.held[0]),)
        elif self.step == 1:
            self.flight = (STAGES[Z1](self.held[0]),)
        elif self.step == 2:
            self.flight = (STAGES[X](self.held[0]), STAGES[Y](self.held[1]))
        else:
            self.flight = (STAGES[Y](self.held[0]), STAGES[X](self.held[1]))

    def finish(self):
        if self.mirrored:
            self.held = (settle(self.held[0], self.flight[0]),)
            self.mirrored, self.flight = False, self.flight[1:]
        if self.native:
            return
        if self.step == 0:
            self.held = (join(self.held[0], self.flight[0], Z2, 1),)
        elif self.step == 1:
            self.held = tuple(join(self.held[0][h], self.flight[0][h], Z1, 1) for h in range(2))
        elif self.step == 2:
            left, right = self.held
            self.held = (join(left, self.flight[0], X, 2), join(right, self.flight[1], Y, 2))
        else:
            left, right = self.held
            self.held = (join(left, self.flight[0], Y, 3), join(right, self.flight[1], X, 2))
        self.flight = ()
        self.step += 1

    def result(self):
        if self.native:
            return tuple(lax.all_gather(self.held[0][k], ("chip", "tensor"), axis=0, tiled=True) for k in range(2))
        return tuple(part.reshape(16 * self.rows, self.width) for part in self.held)


class Reduce:
    def __init__(self, left, right):
        self.width = left.shape[-1]
        self.native = lax.axis_size("chip") != 8
        self.held, self.flight = (left, right), ()
        self.step = 0
        if not self.native:
            self.held = tuple(part.reshape(2, 2, 2, 2, -1, self.width) for part in self.held)

    def start(self):
        if self.native:
            return
        if self.step == 0:
            plan = ((Y, 3), (X, 2))
        elif self.step == 1:
            plan = ((X, 2), (Y, 2))
        elif self.step == 2:
            plan = ((Z1, self.held[0].ndim - 3),)
        else:
            plan = ((Z2, self.held[0].ndim - 3),)
        self.keep, self.flight = [], []
        for part, (stage, axis) in zip(self.held, plan):
            bit = bits()[stage]
            self.keep.append(lax.dynamic_index_in_dim(part, bit, axis, keepdims=False))
            send = lax.dynamic_index_in_dim(part, 1 - bit, axis, keepdims=False)
            if self.step < 3:
                self.flight.append(STAGES[stage](send))
        if self.step == 3:
            self.flight = [cross_far(send), cross(self.keep[0])]
        self.flight = tuple(self.flight)

    def finish(self):
        if self.native:
            return
        if self.step == 3:
            mine = settle(self.keep[0], self.flight[1])
            self.held, self.flight = (mine.astype(jnp.float32) + self.flight[0].astype(jnp.float32),), ()
            return
        total = tuple(
            (mine.astype(jnp.float32) + other.astype(jnp.float32)).astype(jnp.bfloat16)
            for mine, other in zip(self.keep, self.flight)
        )
        self.held = (jnp.stack(total),) if self.step == 1 else total
        self.flight = ()
        self.step += 1

    def result(self):
        if self.native:
            both = jnp.stack(
                [
                    lax.psum_scatter(p, ("chip", "tensor"), scatter_dimension=p.ndim - 2, tiled=True)
                    for p in self.held
                ]
            )
            return settle(both, cross(both)).astype(jnp.float32)
        return self.held[0]


class Sum:
    def __init__(self, values):
        self.native = lax.axis_size("chip") != 8
        if self.native:
            values = lax.psum(values, ("chip", "tensor"))
        self.held, self.flight, self.step = (values,), (), 0

    def start(self):
        if not self.native:
            self.flight = (STAGES[(Z2, Z1, X, Y)[self.step]](self.held[0]),)

    def finish(self):
        if not self.native:
            self.held = (self.held[0] + self.flight[0],)
            self.flight = ()
            self.step += 1


class Order:
    def __init__(self):
        self.now = jnp.zeros((8, 128), jnp.float32)

    def at(self, *values):
        self.now, *values = lax.optimization_barrier((self.now, *values))
        return values

    def follow(self, stream, *values):
        count = len(stream.held)
        out = self.at(*stream.held, *values)
        stream.held = tuple(out[:count])
        return out[count:]

    def arrive(self, streams, *values):
        if not isinstance(streams, tuple):
            streams = (streams,)
        out = self.at(*(part for stream in streams for part in stream.flight), *values)
        for stream in streams:
            count = len(stream.flight)
            stream.flight, out = tuple(out[:count]), out[count:]
            stream.finish()
        return out


def body(
    tokens,
    cotangent,
    segment_ids,
    w_qkv,
    m_qkv,
    a_qkv,
    w_bqv,
    m_bqv,
    a_bqv,
    w_out,
    m_out,
    a_out,
    w_up,
    m_up,
    a_up,
    w_bup,
    m_bup,
    a_bup,
    w_down,
    m_down,
    a_down,
    w_vec,
    m_vec,
    a_vec,
):
    f32, bf16 = jnp.float32, jnp.bfloat16
    core = lax.axis_index("core")
    dev_width = w_bqv.shape[1]
    unit_width = w_bup.shape[0]
    rows = tokens.shape[0]
    half = dev_width // 2
    unit_half = unit_width // 2
    sides = range(2)
    order = Order()

    def pair_dot(lefts, rights, form):
        return sum(jnp.einsum(form, left, right, preferred_element_type=f32) for left, right in zip(lefts, rights))

    def summed(lefts, rights, form):
        away = pair_dot([left[rows:] for left in lefts], rights, form)
        other = core_exchange(away.astype(bf16))
        return pair_dot([left[:rows] for left in lefts], rights, form) + other.astype(f32)

    def full(values):
        return jnp.concatenate([values, core_exchange(values)])

    qkv_shard = w_qkv.astype(bf16)
    qkv_own = jnp.stack(
        [jnp.concatenate([qkv_shard[k, :, h * half : (h + 1) * half] for k in range(3)], 1) for h in sides]
    )
    qkv_own, tokens, cotangent = order.at(qkv_own, tokens, cotangent)
    qkv = Gather((qkv_own,), mirrored=True)
    qkv.start()
    out_shard, up_shard, down_shard = w_out.T.astype(bf16), w_up.astype(bf16), w_down.T.astype(bf16)
    rest = jnp.stack(
        [
            jnp.concatenate(
                [
                    out_shard[:, h * half : (h + 1) * half],
                    up_shard[:, h * unit_half : (h + 1) * unit_half],
                    down_shard[:, h * unit_half : (h + 1) * unit_half],
                ],
                1,
            )
            for h in sides
        ]
    )
    small = jnp.concatenate([w_bqv.reshape(-1), w_bup, segment_ids.reshape(-1).astype(f32)])
    rest, tokens = order.at(rest, tokens)
    rest_other = cross(rest)
    (tokens, small) = order.arrive(qkv, tokens, small)
    qkv.start()
    tok_other = cross(tokens)
    (rest_other, small) = order.arrive(qkv, rest_other, small)
    qkv.start()
    small_other = cross(small)
    upo, down = Gather((settle(rest, rest_other),)).fork(half + unit_half)
    upo.start()
    (tok_other,) = order.arrive((qkv, upo), tok_other)
    qkv.start()
    upo.start()
    tokens = settle(tokens, tok_other)
    tok_far = core_exchange(tokens)
    tok_far, small_other = order.at(tok_far, small_other)
    small = settle(small, small_other)
    b_qv = small[: 2 * dev_width].reshape(2, dev_width)
    b_up = small[2 * dev_width : 2 * dev_width + unit_width]
    segments = small[2 * dev_width + unit_width :].astype(jnp.int32).reshape(1, -1)
    segments = jnp.where(core == 1, jnp.roll(segments, rows, axis=1), segments)
    seg_col = segments.reshape(-1, 1)
    tok_full = jnp.concatenate([tokens, tok_far])
    (tok_full, seg_col, cotangent, *down.held) = order.arrive((upo, qkv), tok_full, seg_col, cotangent, *down.held)
    (tok_full,) = order.follow(upo, tok_full)
    upo.start()
    down.start()
    cot_other = cross(cotangent)
    qkv_w = qkv.result()

    packed, context, logsum = [], [], []
    for h in sides:
        bias = jnp.concatenate(
            [b_qv[0, h * half : (h + 1) * half], jnp.zeros((half,), f32), b_qv[1, h * half : (h + 1) * half]]
        )
        packed.append((jnp.dot(tok_full, qkv_w[h], preferred_element_type=f32) + bias).astype(bf16))
    for h in sides:
        ctx, lse = attend_forward(packed[h], seg_col)
        context.append(ctx)
        logsum.append(lse)
        if h == 0:
            (context[0], packed[1]) = order.arrive(upo, context[0], packed[1])
            (packed[1],) = order.follow(upo, packed[1])
            upo.start()
    (cot_other, *context) = order.arrive(down, cot_other, *context)
    down.start()
    cotangent = settle(cotangent, cot_other)
    order.arrive(down)
    down.start()
    context = order.arrive((upo, down), *context)
    context = order.follow(down, *context)
    down.start()
    uo_w = upo.result()
    out_w = [part[:, :half] for part in uo_w]
    up_w = [part[:, half:] for part in uo_w]

    attended = summed(context, out_w, "ne,de->nd")
    first_sum = tokens.astype(f32) + attended + w_vec[0]
    hidden, first_pull = jax.vjp(layer_norm, first_sum, w_vec[2], w_vec[3])
    hidden_full = full(hidden.astype(bf16))
    active16, gelu_pulls = [], []
    for h in sides:
        upper = jnp.dot(hidden_full, up_w[h], preferred_element_type=f32) + b_up[h * unit_half : (h + 1) * unit_half]
        active, pull = jax.vjp(gelu_exact, upper)
        active16.append(active.astype(bf16))
        gelu_pulls.append(pull)
    active16 = order.arrive(down, *active16)
    down_w = down.result()
    mixed = summed(active16, down_w, "nf,df->nd")
    second_sum = hidden + mixed + w_vec[1]
    normed, second_pull = jax.vjp(layer_norm, second_sum, w_vec[4], w_vec[5])
    layer_out = normed.astype(bf16)
    second_grad, gain2_grad, shift2_grad = second_pull(cotangent.astype(f32))
    second_far = core_exchange(second_grad.astype(bf16))
    (second_far, layer_out) = order.at(second_far, layer_out)
    out_other = cross(layer_out)
    second_full = jnp.concatenate([second_grad.astype(bf16), second_far])
    down_grads = [jnp.einsum("nd,nf->df", second_full, active16[h], preferred_element_type=f32).astype(bf16) for h in sides]
    (second_full, out_other, *down_grads) = order.at(second_full, out_other, *down_grads)
    down_sum = Reduce(*down_grads)
    down_sum.start()
    upper_grads, upper16, up_grads = [], [], []
    for h in sides:
        active_grad = jnp.einsum("nd,df->nf", second_full, down_w[h], preferred_element_type=f32)
        upper_grads.append(gelu_pulls[h](active_grad)[0])
        upper16.append(upper_grads[h].astype(bf16))
    for h in sides:
        up_grads.append(jnp.einsum("nd,nf->df", hidden_full, upper16[h], preferred_element_type=f32).astype(bf16))
    (upper16[0], upper16[1], *up_grads) = order.arrive(down_sum, *upper16, *up_grads)
    down_sum.start()
    hidden_grad = second_grad + summed(upper16, up_w, "nf,df->nd")
    first_grad, gain1_grad, shift1_grad = first_pull(hidden_grad)
    first_full = full(first_grad.astype(bf16))
    out_grads = [jnp.einsum("nd,ne->de", first_full, context[h], preferred_element_type=f32).astype(bf16) for h in sides]
    uo_grads = [jnp.concatenate([out_grads[h], up_grads[h]], 1) for h in sides]
    (first_full, *uo_grads) = order.at(first_full, *uo_grads)
    upo_sum = Reduce(*uo_grads)
    upo_sum.start()
    context_grads = [
        jnp.einsum("nd,de->ne", first_full, out_w[h], preferred_element_type=f32).astype(bf16) for h in sides
    ]
    context_grads = order.arrive(down_sum, *context_grads)
    down_sum.start()
    packed16, bias_sums = [None, None], [None, None]
    packed16[0], bias_sums[0] = attend_backward(packed[0], context_grads[0], context[0], logsum[0], seg_col)
    (context_grads[1], packed16[0]) = order.arrive(down_sum, context_grads[1], packed16[0])
    layer_out = settle(layer_out, out_other)
    down_sum.start()
    (context_grads[1], packed16[0]) = order.arrive(upo_sum, context_grads[1], packed16[0])
    upo_sum.start()
    vec_local = jnp.stack(
        [
            jnp.sum(first_grad, axis=0),
            jnp.sum(second_grad, axis=0),
            gain1_grad,
            shift1_grad,
            gain2_grad,
            shift2_grad,
        ]
    )
    bup_local = jnp.concatenate([jnp.sum(part, axis=0) for part in upper_grads])
    vec_far = core_exchange(vec_local)
    packed16[1], bias_sums[1] = attend_backward(packed[1], context_grads[1], context[1], logsum[1], seg_col)
    qkv_grads = [jnp.einsum("nd,ne->de", tok_full, packed16[h], preferred_element_type=f32).astype(bf16) for h in sides]
    out = order.arrive((down_sum, upo_sum), vec_far, *packed16, *qkv_grads)
    vec_far, packed16, qkv_grads = out[0], out[1:3], out[3:]
    qkv_sum = Reduce(*qkv_grads)
    qkv_sum.start()
    packed16 = order.follow(upo_sum, *packed16)
    upo_sum.start()
    bqv_local = jnp.concatenate(bias_sums, 1)
    totals = Sum(jnp.concatenate([(vec_local + vec_far).reshape(-1), bqv_local.reshape(-1), bup_local]))
    totals.start()
    down_both = down_sum.result()
    away = pair_dot([part[rows:] for part in packed16], qkv_w, "ne,de->nd")
    grad_far = core_exchange(away.astype(bf16))
    packed16 = order.arrive((upo_sum, totals), *packed16)
    upo_sum.start()
    totals.start()
    near = pair_dot([part[:rows] for part in packed16], qkv_w, "ne,de->nd")
    grad_tokens = (first_grad + near + grad_far.astype(f32)).astype(bf16)
    (grad_tokens, down_both) = order.arrive(totals, grad_tokens, down_both)
    totals.start()
    order.arrive(qkv_sum)
    qkv_sum.start()
    order.arrive((upo_sum, totals))
    totals.start()
    upo_both = upo_sum.result()
    (upo_both, grad_tokens) = order.arrive(qkv_sum, upo_both, grad_tokens)
    qkv_sum.start()
    grad_other = cross(grad_tokens)
    order.arrive(totals)
    vectors = totals.held[0]
    count = vec_local.size
    vec_grad = vectors[:count].reshape(vec_local.shape)
    tail = vectors[count:]
    tail_other = cross(tail)
    order.arrive(qkv_sum)
    qkv_sum.start()
    (tail_other, grad_other) = order.at(tail_other, grad_other)
    order.arrive(qkv_sum)
    qkv_both = qkv_sum.result()
    tail = settle(tail, tail_other)
    bqv_grad = tail[: bqv_local.size].reshape(bqv_local.shape)
    bup_grad = tail[bqv_local.size :]
    grad_tokens = settle(grad_tokens, grad_other)
    (vec_grad,) = order.at(vec_grad)
    vec_grad = vec_grad + order.now[0, 0]
    qkv_part = jnp.stack(
        [jnp.concatenate([qkv_both[h, :, k * half : (k + 1) * half] for h in sides], 1) for k in range(3)]
    )
    out_part = jnp.concatenate([upo_both[h, :, :half] for h in sides], 1).T
    up_part = jnp.concatenate([upo_both[h, :, half:] for h in sides], 1)
    down_part = jnp.concatenate([down_both[h] for h in sides], 1).T
    base_rate = 1.0 / math.sqrt(SEQ_LEN * lax.axis_size(("chip", "core")))
    slow_rate = MATRIX_RATE * base_rate
    fast_rate = FASTER_RATE * base_rate
    nm_qkv, nw_qkv, na_qkv = advance(w_qkv, m_qkv, a_qkv, qkv_part, slow_rate)
    nm_bqv, nw_bqv, na_bqv = advance(w_bqv, m_bqv, a_bqv, bqv_grad, slow_rate)
    nm_out, nw_out, na_out = advance(w_out, m_out, a_out, out_part, fast_rate)
    nm_up, nw_up, na_up = advance(w_up, m_up, a_up, up_part, slow_rate)
    nm_bup, nw_bup, na_bup = advance(w_bup, m_bup, a_bup, bup_grad, fast_rate)
    nm_down, nw_down, na_down = advance(w_down, m_down, a_down, down_part, slow_rate)
    nm_vec, nw_vec, na_vec = advance(w_vec, m_vec, a_vec, vec_grad, slow_rate)
    return (
        layer_out,
        grad_tokens,
        nm_qkv,
        nw_qkv,
        na_qkv,
        nm_bqv,
        nw_bqv,
        na_bqv,
        nm_out,
        nw_out,
        na_out,
        nm_up,
        nw_up,
        na_up,
        nm_bup,
        nw_bup,
        na_bup,
        nm_down,
        nw_down,
        na_down,
        nm_vec,
        nw_vec,
        na_vec,
    )


def solution(mesh):
    devices = mesh.devices.reshape(-1, 2, 2)
    split_mesh = Mesh(devices, ("chip", "core", "tensor"))
    dp = ("chip", "core")
    row = P(("chip", "core", "tensor"), None)
    deep = P(None, dp, "tensor")
    wide = P("tensor", dp)
    tall = P(dp, "tensor")
    qv = P(None, "tensor")
    unit = P("tensor")
    in_specs = (row, row, P(dp, None)) + (deep,) * 3 + (qv,) * 3 + (wide,) * 3 + (tall,) * 3 + (unit,) * 3 + (wide,) * 3 + (P(),) * 3
    out_specs = (row, row) + in_specs[3:]
    return jax.shard_map(body, mesh=split_mesh, in_specs=in_specs, out_specs=out_specs, check_vma=False)
```

```python
import functools
import math

import jax
import jax.numpy as jnp
from jax import lax
from jax.experimental import pallas as pl
from jax.experimental.pallas import tpu as pltpu
from jax.sharding import Mesh, PartitionSpec as P

HEAD_DIM = 64
SEQ_LEN = 1024


NORM_EPS = 1e-05
MOMENTUM = 0.9
AVERAGE = 0.75
MATRIX_RATE = 0.05
FASTER_RATE = 0.25


def layer_norm(values, gain, shift):
    centred = values - jnp.mean(values, axis=-1, keepdims=True)
    spread = jnp.mean(centred * centred, axis=-1, keepdims=True)
    return centred * lax.rsqrt(spread + NORM_EPS) * gain + shift


def gelu_exact(values):
    return jax.nn.gelu(values, approximate=False)


def advance(weight, moment, average, gradient, step_rate):
    new_moment = MOMENTUM * moment + gradient
    new_weight = weight - step_rate * (gradient + MOMENTUM * new_moment)
    new_average = AVERAGE * average + (1.0 - AVERAGE) * new_weight
    return (new_moment, new_weight, new_average)


NT = (((1,), (1,)), ((), ()))
TN = (((0,), (0,)), ((), ()))
FAR = -1e30


def dot32(left, right, dims=(((1,), (0,)), ((), ()))):
    return lax.dot_general(left, right, dims, preferred_element_type=jnp.float32)


def three_terms(values):
    high = values.astype(jnp.bfloat16).astype(jnp.float32)
    rest = values - high
    middle = rest.astype(jnp.bfloat16).astype(jnp.float32)
    return (high, middle, rest - middle)


def place(lane, terms, other):
    high, middle, low = terms
    return jnp.where(lane == 63, high, jnp.where(lane == 62, middle, jnp.where(lane == 61, low, other)))


def forward_kernel(q_ref, k_ref, v_ref, seg_ref, out_ref, lse_ref, *, block):
    f32, bf16 = jnp.float32, jnp.bfloat16
    rows = q_ref.shape[0]
    lanes = lax.broadcasted_iota(jnp.int32, (rows, 128), 1)
    lower = lanes < HEAD_DIM
    lane = lanes & 63
    same = lane == seg_ref[...]
    q_mark = jnp.where(same, 1.0, 0.0)
    k_mark = jnp.where(same, 0.0, FAR)
    query = q_ref[...].astype(f32)
    keys = k_ref[...].astype(f32) * 0.125
    value = v_ref[...].astype(f32)
    q_heads = [jnp.where(lower, query, q_mark).astype(bf16), jnp.where(lower, q_mark, query).astype(bf16)]
    k_heads = [jnp.where(lower, keys, k_mark).astype(bf16), jnp.where(lower, k_mark, keys).astype(bf16)]
    v_heads = [jnp.where(lower, value, 1.0).astype(bf16), jnp.where(lower, 1.0, value).astype(bf16)]
    low = lower[:block]
    for start in range(0, rows, block):
        parts = []
        for head in range(2):
            scores = dot32(q_heads[head][start : start + block], k_heads[head], NT)
            top = jnp.max(scores, axis=1, keepdims=True)
            weights = jnp.exp(scores - top).astype(bf16)
            parts.append((dot32(weights, v_heads[head]), top))
        (first, top0), (second, top1) = parts
        total = pltpu.roll(jnp.where(low, second, first), HEAD_DIM, 1)
        out_ref[start : start + block, :] = (jnp.where(low, first, second) / total).astype(bf16)
        lse_ref[start : start + block, :] = jnp.where(low, top0, top1) + jnp.log(total)


def backward_kernel(q_ref, k_ref, v_ref, g_ref, o_ref, lse_ref, seg_ref, d_ref, sum_ref, *, block):
    f32, bf16 = jnp.float32, jnp.bfloat16
    rows = q_ref.shape[0]
    lanes = lax.broadcasted_iota(jnp.int32, (rows, 128), 1)
    lower = lanes < HEAD_DIM
    lane = lanes & 63
    same = lane == seg_ref[...]
    query = q_ref[...].astype(f32)
    keys = k_ref[...].astype(f32) * 0.125
    value = v_ref[...].astype(f32)
    grad = g_ref[...].astype(f32)
    lse = pltpu.roll(lse_ref[...], HEAD_DIM, 1)
    q_mark = place(lane, three_terms(-lse), jnp.where(same, 1.0, 0.0))
    k_mark = jnp.where(lane > 60, 1.0, jnp.where(same, 0.0, FAR))
    inner = grad * o_ref[...].astype(f32)
    inner0 = jnp.sum(jnp.where(lower, inner, 0.0), axis=1, keepdims=True)
    inner1 = jnp.sum(jnp.where(lower, 0.0, inner), axis=1, keepdims=True)
    g_mark = place(lane, three_terms(-jnp.where(lower, inner1, inner0)), 0.0)
    v_mark = jnp.where(lane > 60, 1.0, 0.0)

    def heads(values, mark):
        return [jnp.where(lower, values, mark).astype(bf16), jnp.where(lower, mark, values).astype(bf16)]

    q_heads, k_heads = heads(query, q_mark), heads(keys, k_mark)
    v_heads, g_heads = heads(value, v_mark), heads(grad, g_mark)
    q_small = (query * 0.125).astype(bf16)
    k_small = keys.astype(bf16)
    grad16 = g_ref[...]
    low = lower[:block]
    q_grads = [None, None]
    spot = pl.program_id(0) * 128
    places = [pl.ds(pl.multiple_of(k * (d_ref.shape[1] // 3) + spot, 128), 128) for k in range(3)]
    v_sum = jnp.zeros((1, 128), f32)
    for start in range(0, rows, block):
        stop = start + block
        dv, dk = [], []
        for head in range(2):
            probs = jnp.exp(dot32(k_heads[head][start:stop], q_heads[head], NT))
            delta = dot32(v_heads[head][start:stop], g_heads[head], NT)
            dv.append(dot32(probs.astype(bf16), grad16))
            change = (probs * delta).astype(bf16)
            dk.append(dot32(change, q_small))
            part = dot32(change, k_small[start:stop], TN)
            q_grads[head] = part if q_grads[head] is None else q_grads[head] + part
        v_grad = jnp.where(low, dv[0], dv[1])
        v_sum = v_sum + jnp.sum(v_grad, axis=0, keepdims=True)
        d_ref[start:stop, places[1]] = jnp.where(low, dk[0], dk[1]).astype(bf16)
        d_ref[start:stop, places[2]] = v_grad.astype(bf16)
    q_grad = jnp.where(lower, q_grads[0], q_grads[1])
    d_ref[:, places[0]] = q_grad.astype(bf16)
    sum_ref[0:1, :] = jnp.sum(q_grad, axis=0, keepdims=True)
    sum_ref[1:2, :] = v_sum


def part_specs(rows, pairs):
    return [pl.BlockSpec((rows, 128), lambda i, k=k: (0, k * pairs + i)) for k in range(3)]


def attend_forward(packed, seg_col, block=512):
    rows, width = packed.shape
    pairs = width // 384
    flat = pl.BlockSpec((rows, 128), lambda i: (0, i))
    return pl.pallas_call(
        functools.partial(forward_kernel, block=block),
        grid=(pairs,),
        in_specs=part_specs(rows, pairs) + [pl.BlockSpec((rows, 1), lambda i: (0, 0))],
        out_specs=[flat, flat],
        out_shape=[
            jax.ShapeDtypeStruct((rows, pairs * 128), jnp.bfloat16),
            jax.ShapeDtypeStruct((rows, pairs * 128), jnp.float32),
        ],
        compiler_params=pltpu.CompilerParams(vmem_limit_bytes=48 * 2**20),
        name="attend_forward",
    )(packed, packed, packed, seg_col)


def attend_backward(packed, grad, context, lse, seg_col, block=256):
    rows, width = packed.shape
    pairs = width // 384
    flat = pl.BlockSpec((rows, 128), lambda i: (0, i))
    return pl.pallas_call(
        functools.partial(backward_kernel, block=block),
        grid=(pairs,),
        in_specs=part_specs(rows, pairs) + [flat] * 3 + [pl.BlockSpec((rows, 1), lambda i: (0, 0))],
        out_specs=[
            pl.BlockSpec((rows, width), lambda i: (0, 0)),
            pl.BlockSpec((2, 128), lambda i: (0, i)),
        ],
        out_shape=[
            jax.ShapeDtypeStruct((rows, width), jnp.bfloat16),
            jax.ShapeDtypeStruct((2, pairs * 128), jnp.float32),
        ],
        compiler_params=pltpu.CompilerParams(vmem_limit_bytes=48 * 2**20),
        name="attend_backward",
    )(packed, packed, packed, grad, context, lse, seg_col)


CROSS = [(1, 2), (2, 1)]
FLIP = [(0, 1), (1, 0)]


def cross(values):
    return lax.ppermute(values, ("core", "tensor"), CROSS)


def cross_far(values):
    pairs = []
    for chip in range(lax.axis_size("chip")):
        for core in range(2):
            for side in range(2):
                pairs.append((chip * 4 + core * 2 + side, (chip ^ 4) * 4 + side * 2 + core))
    return lax.ppermute(values, ("chip", "core", "tensor"), pairs)


def settle(mine, other):
    return jnp.where(lax.axis_index("core") == lax.axis_index("tensor"), mine, other)


def core_exchange(values):
    return lax.ppermute(values, "core", FLIP)


def y_exchange(values):
    return lax.ppermute(values, "tensor", FLIP)


def chip_exchange(values, mask):
    count = lax.axis_size("chip")
    return lax.ppermute(values, "chip", [(k, k ^ mask) for k in range(count)])


def bits():
    chip = lax.axis_index("chip")
    return (lax.axis_index("tensor"), chip & 1, (chip >> 1) & 1, (chip >> 2) & 1)


STAGES = (
    y_exchange,
    lambda values: chip_exchange(values, 1),
    lambda values: chip_exchange(values, 2),
    lambda values: chip_exchange(values, 4),
)
Y, X, Z1, Z2 = range(4)


def join(mine, other, stage, axis):
    first = bits()[stage] == 0
    return jnp.where(first, jnp.stack([mine, other], axis), jnp.stack([other, mine], axis))


class Gather:
    def __init__(self, held, step=0, mirrored=False):
        self.mirrored = mirrored
        self.rows, self.width = held[0].shape[-2:]
        self.native = lax.axis_size("chip") != 8
        self.flight = ()
        self.held = held
        self.step = step

    def fork(self, width):
        return (
            Gather(tuple(part[..., :width] for part in self.held), self.step),
            Gather(tuple(part[..., width:] for part in self.held), self.step),
        )

    def start(self):
        if self.mirrored:
            far = () if self.native else (cross_far(self.held[0]),)
            self.flight = (cross(self.held[0]),) + far
        elif self.native:
            return
        elif self.step == 0:
            self.flight = (STAGES[Z2](self.held[0]),)
        elif self.step == 1:
            self.flight = (STAGES[Z1](self.held[0]),)
        elif self.step == 2:
            self.flight = (STAGES[X](self.held[0]), STAGES[Y](self.held[1]))
        else:
            self.flight = (STAGES[Y](self.held[0]), STAGES[X](self.held[1]))

    def finish(self):
        if self.mirrored:
            self.held = (settle(self.held[0], self.flight[0]),)
            self.mirrored, self.flight = False, self.flight[1:]
        if self.native:
            return
        if self.step == 0:
            self.held = (join(self.held[0], self.flight[0], Z2, 1),)
        elif self.step == 1:
            self.held = tuple(join(self.held[0][h], self.flight[0][h], Z1, 1) for h in range(2))
        elif self.step == 2:
            left, right = self.held
            self.held = (join(left, self.flight[0], X, 2), join(right, self.flight[1], Y, 2))
        else:
            left, right = self.held
            self.held = (join(left, self.flight[0], Y, 3), join(right, self.flight[1], X, 2))
        self.flight = ()
        self.step += 1

    def result(self):
        if self.native:
            return tuple(lax.all_gather(self.held[0][k], ("chip", "tensor"), axis=0, tiled=True) for k in range(2))
        return tuple(part.reshape(16 * self.rows, self.width) for part in self.held)


class Reduce:
    def __init__(self, left, right):
        self.width = left.shape[-1]
        self.native = lax.axis_size("chip") != 8
        self.held, self.flight = (left, right), ()
        self.step = 0
        if not self.native:
            self.held = tuple(part.reshape(2, 2, 2, 2, -1, self.width) for part in self.held)

    def start(self, order=None, *values):
        if self.native:
            return values
        if self.step == 0:
            plan = ((Y, 3), (X, 2))
        elif self.step == 1:
            plan = ((X, 2), (Y, 2))
        elif self.step == 2:
            plan = ((Z1, self.held[0].ndim - 3),)
        else:
            plan = ((Z2, self.held[0].ndim - 3),)
        self.keep, sends = [], []
        for part, (stage, axis) in zip(self.held, plan):
            bit = bits()[stage]
            self.keep.append(lax.dynamic_index_in_dim(part, bit, axis, keepdims=False))
            sends.append(lax.dynamic_index_in_dim(part, 1 - bit, axis, keepdims=False))
        if order is not None:
            out = order.at(*sends, *values)
            sends, values = out[: len(sends)], out[len(sends) :]
        if self.step == 3:
            self.flight = (cross_far(sends[0]), cross(self.keep[0]))
        else:
            self.flight = tuple(STAGES[stage](send) for send, (stage, _) in zip(sends, plan))
        return values

    def finish(self):
        if self.native:
            return
        if self.step == 3:
            mine = settle(self.keep[0], self.flight[1])
            self.held, self.flight = (mine.astype(jnp.float32) + self.flight[0].astype(jnp.float32),), ()
            return
        total = tuple(
            (mine.astype(jnp.float32) + other.astype(jnp.float32)).astype(jnp.bfloat16)
            for mine, other in zip(self.keep, self.flight)
        )
        self.held = (jnp.stack(total),) if self.step == 1 else total
        self.flight = ()
        self.step += 1

    def result(self):
        if self.native:
            both = jnp.stack(
                [
                    lax.psum_scatter(p, ("chip", "tensor"), scatter_dimension=p.ndim - 2, tiled=True)
                    for p in self.held
                ]
            )
            return settle(both, cross(both)).astype(jnp.float32)
        return self.held[0]


class Sum:
    def __init__(self, values):
        self.native = lax.axis_size("chip") != 8
        if self.native:
            values = lax.psum(values, ("chip", "tensor"))
        self.held, self.flight, self.step = (values,), (), 0

    def start(self):
        if not self.native:
            self.flight = (STAGES[(Z2, Z1, X, Y)[self.step]](self.held[0]),)

    def finish(self):
        if not self.native:
            self.held = (self.held[0] + self.flight[0],)
            self.flight = ()
            self.step += 1


class Order:
    def __init__(self):
        self.now = jnp.zeros((8, 128), jnp.float32)

    def at(self, *values):
        self.now, *values = lax.optimization_barrier((self.now, *values))
        return values

    def follow(self, stream, *values):
        count = len(stream.held)
        out = self.at(*stream.held, *values)
        stream.held = tuple(out[:count])
        return out[count:]

    def arrive(self, streams, *values):
        if not isinstance(streams, tuple):
            streams = (streams,)
        out = self.at(*(part for stream in streams for part in stream.flight), *values)
        for stream in streams:
            count = len(stream.flight)
            stream.flight, out = tuple(out[:count]), out[count:]
            stream.finish()
        return out


def body(
    tokens,
    cotangent,
    segment_ids,
    w_qkv,
    m_qkv,
    a_qkv,
    w_bqv,
    m_bqv,
    a_bqv,
    w_out,
    m_out,
    a_out,
    w_up,
    m_up,
    a_up,
    w_bup,
    m_bup,
    a_bup,
    w_down,
    m_down,
    a_down,
    w_vec,
    m_vec,
    a_vec,
):
    f32, bf16 = jnp.float32, jnp.bfloat16
    core = lax.axis_index("core")
    dev_width = w_bqv.shape[1]
    unit_width = w_bup.shape[0]
    rows = tokens.shape[0]
    half = dev_width // 2
    unit_half = unit_width // 2
    sides = range(2)
    order = Order()

    def pair_dot(lefts, rights, form):
        return sum(jnp.einsum(form, left, right, preferred_element_type=f32) for left, right in zip(lefts, rights))

    def summed(lefts, rights, form):
        away = pair_dot([left[rows:] for left in lefts], rights, form)
        other = core_exchange(away.astype(bf16))
        return pair_dot([left[:rows] for left in lefts], rights, form) + other.astype(f32)

    def full(values):
        return jnp.concatenate([values, core_exchange(values)])

    qkv_shard = w_qkv.astype(bf16)
    qkv_own = jnp.stack(
        [jnp.concatenate([qkv_shard[k, :, h * half : (h + 1) * half] for k in range(3)], 1) for h in sides]
    )
    qkv_own, tokens, cotangent = order.at(qkv_own, tokens, cotangent)
    qkv = Gather((qkv_own,), mirrored=True)
    qkv.start()
    out_shard, up_shard, down_shard = w_out.T.astype(bf16), w_up.astype(bf16), w_down.T.astype(bf16)
    rest = jnp.stack(
        [
            jnp.concatenate(
                [
                    out_shard[:, h * half : (h + 1) * half],
                    up_shard[:, h * unit_half : (h + 1) * unit_half],
                    down_shard[:, h * unit_half : (h + 1) * unit_half],
                ],
                1,
            )
            for h in sides
        ]
    )
    small = jnp.concatenate([w_bqv.reshape(-1), w_bup, segment_ids.reshape(-1).astype(f32)])
    rest, tokens = order.at(rest, tokens)
    rest_other = cross(rest)
    (tokens, small) = order.arrive(qkv, tokens, small)
    qkv.start()
    tok_other = cross(tokens)
    (rest_other, small) = order.arrive(qkv, rest_other, small)
    qkv.start()
    small_other = cross(small)
    upo, down = Gather((settle(rest, rest_other),)).fork(half + unit_half)
    upo.start()
    (tok_other,) = order.arrive((qkv, upo), tok_other)
    qkv.start()
    upo.start()
    tokens = settle(tokens, tok_other)
    tok_far = core_exchange(tokens)
    tok_far, small_other = order.at(tok_far, small_other)
    small = settle(small, small_other)
    b_qv = small[: 2 * dev_width].reshape(2, dev_width)
    b_up = small[2 * dev_width : 2 * dev_width + unit_width]
    segments = small[2 * dev_width + unit_width :].astype(jnp.int32).reshape(1, -1)
    segments = jnp.where(core == 1, jnp.roll(segments, rows, axis=1), segments)
    seg_col = segments.reshape(-1, 1)
    tok_full = jnp.concatenate([tokens, tok_far])
    (tok_full, seg_col, cotangent, *down.held) = order.arrive((upo, qkv), tok_full, seg_col, cotangent, *down.held)
    (tok_full,) = order.follow(upo, tok_full)
    upo.start()
    down.start()
    cot_other = cross(cotangent)
    qkv_w = qkv.result()

    packed, context, logsum = [], [], []
    for h in sides:
        bias = jnp.concatenate(
            [b_qv[0, h * half : (h + 1) * half], jnp.zeros((half,), f32), b_qv[1, h * half : (h + 1) * half]]
        )
        packed.append((jnp.dot(tok_full, qkv_w[h], preferred_element_type=f32) + bias).astype(bf16))
    for h in sides:
        ctx, lse = attend_forward(packed[h], seg_col)
        context.append(ctx)
        logsum.append(lse)
        if h == 0:
            (context[0], packed[1]) = order.arrive(upo, context[0], packed[1])
            (packed[1],) = order.follow(upo, packed[1])
            upo.start()
    (cot_other, *context) = order.arrive(down, cot_other, *context)
    down.start()
    cotangent = settle(cotangent, cot_other)
    order.arrive(down)
    down.start()
    context = order.arrive(upo, *context)
    uo_w = upo.result()
    out_w = [part[:, :half] for part in uo_w]
    up_w = [part[:, half:] for part in uo_w]

    attended = summed(context, out_w, "ne,de->nd")
    (attended,) = order.arrive(down, attended)
    down.start()
    first_sum = tokens.astype(f32) + attended + w_vec[0]
    hidden, first_pull = jax.vjp(layer_norm, first_sum, w_vec[2], w_vec[3])
    hidden_full = full(hidden.astype(bf16))
    active16, gelu_pulls = [], []
    for h in sides:
        upper = jnp.dot(hidden_full, up_w[h], preferred_element_type=f32) + b_up[h * unit_half : (h + 1) * unit_half]
        active, pull = jax.vjp(gelu_exact, upper)
        active16.append(active.astype(bf16))
        gelu_pulls.append(pull)
    active16 = order.arrive(down, *active16)
    down_w = down.result()
    mixed = summed(active16, down_w, "nf,df->nd")
    second_sum = hidden + mixed + w_vec[1]
    normed, second_pull = jax.vjp(layer_norm, second_sum, w_vec[4], w_vec[5])
    layer_out = normed.astype(bf16)
    second_grad, gain2_grad, shift2_grad = second_pull(cotangent.astype(f32))
    second_far = core_exchange(second_grad.astype(bf16))
    (second_far, layer_out) = order.at(second_far, layer_out)
    out_other = cross(layer_out)
    second_full = jnp.concatenate([second_grad.astype(bf16), second_far])
    down_grads = [jnp.einsum("nd,nf->df", second_full, active16[h], preferred_element_type=f32).astype(bf16) for h in sides]
    (second_full, out_other, *down_grads) = order.at(second_full, out_other, *down_grads)
    down_sum = Reduce(*down_grads)
    down_sum.start()
    upper_grads, upper16, up_grads = [], [], []
    for h in sides:
        active_grad = jnp.einsum("nd,df->nf", second_full, down_w[h], preferred_element_type=f32)
        upper_grads.append(gelu_pulls[h](active_grad)[0])
        upper16.append(upper_grads[h].astype(bf16))
    for h in sides:
        up_grads.append(jnp.einsum("nd,nf->df", hidden_full, upper16[h], preferred_element_type=f32).astype(bf16))
    (upper16[0], upper16[1], *up_grads) = order.arrive(down_sum, *upper16, *up_grads)
    down_sum.start()
    hidden_grad = second_grad + summed(upper16, up_w, "nf,df->nd")
    first_grad, gain1_grad, shift1_grad = first_pull(hidden_grad)
    first_full = full(first_grad.astype(bf16))
    out_grads = [jnp.einsum("nd,ne->de", first_full, context[h], preferred_element_type=f32).astype(bf16) for h in sides]
    uo_grads = [jnp.concatenate([out_grads[h], up_grads[h]], 1) for h in sides]
    (first_full, *uo_grads) = order.at(first_full, *uo_grads)
    upo_sum = Reduce(*uo_grads)
    (first_full,) = upo_sum.start(order, first_full)
    context_grads = [
        jnp.einsum("nd,de->ne", first_full, out_w[h], preferred_element_type=f32).astype(bf16) for h in sides
    ]
    context_grads = order.arrive(down_sum, *context_grads)
    down_sum.start()
    packed16, bias_sums = [None, None], [None, None]
    packed16[0], bias_sums[0] = attend_backward(packed[0], context_grads[0], context[0], logsum[0], seg_col)
    (context_grads[1], packed16[0]) = order.arrive(down_sum, context_grads[1], packed16[0])
    down_sum.start()
    (context_grads[1], packed16[0]) = order.arrive(upo_sum, context_grads[1], packed16[0])
    upo_sum.start()
    vec_local = jnp.stack(
        [
            jnp.sum(first_grad, axis=0),
            jnp.sum(second_grad, axis=0),
            gain1_grad,
            shift1_grad,
            gain2_grad,
            shift2_grad,
        ]
    )
    bup_local = jnp.concatenate([jnp.sum(part, axis=0) for part in upper_grads])
    vec_far = core_exchange(vec_local)
    packed16[1], bias_sums[1] = attend_backward(packed[1], context_grads[1], context[1], logsum[1], seg_col)
    qkv_grads = [jnp.einsum("nd,ne->de", tok_full, packed16[h], preferred_element_type=f32).astype(bf16) for h in sides]
    out = order.arrive((down_sum, upo_sum), vec_far, *packed16, *qkv_grads)
    vec_far, packed16, qkv_grads = out[0], out[1:3], out[3:]
    qkv_sum = Reduce(*qkv_grads)
    qkv_sum.start()
    packed16 = order.follow(upo_sum, *packed16)
    upo_sum.start()
    bqv_local = jnp.concatenate(bias_sums, 1)
    totals = Sum(jnp.concatenate([(vec_local + vec_far).reshape(-1), bqv_local.reshape(-1), bup_local]))
    totals.start()
    down_both = down_sum.result()
    away = pair_dot([part[rows:] for part in packed16], qkv_w, "ne,de->nd")
    grad_far = core_exchange(away.astype(bf16))
    packed16 = order.arrive((upo_sum, totals), *packed16)
    upo_sum.start()
    totals.start()
    near = pair_dot([part[:rows] for part in packed16], qkv_w, "ne,de->nd")
    grad_tokens = (first_grad + near + grad_far.astype(f32)).astype(bf16)
    (grad_tokens, down_both) = order.arrive(totals, grad_tokens, down_both)
    totals.start()
    (layer_out, out_other) = order.arrive(qkv_sum, layer_out, out_other)
    qkv_sum.start()
    layer_out = settle(layer_out, out_other)
    order.arrive((upo_sum, totals))
    totals.start()
    upo_both = upo_sum.result()
    (upo_both, grad_tokens) = order.arrive(qkv_sum, upo_both, grad_tokens)
    qkv_sum.start()
    grad_other = cross(grad_tokens)
    order.arrive(totals)
    vectors = totals.held[0]
    count = vec_local.size
    vec_grad = vectors[:count].reshape(vec_local.shape)
    tail = vectors[count:]
    tail_other = cross(tail)
    order.arrive(qkv_sum)
    qkv_sum.start()
    (tail_other, grad_other) = order.at(tail_other, grad_other)
    order.arrive(qkv_sum)
    qkv_both = qkv_sum.result()
    tail = settle(tail, tail_other)
    bqv_grad = tail[: bqv_local.size].reshape(bqv_local.shape)
    bup_grad = tail[bqv_local.size :]
    grad_tokens = settle(grad_tokens, grad_other)
    (vec_grad,) = order.at(vec_grad)
    vec_grad = vec_grad + order.now[0, 0]
    qkv_part = jnp.stack(
        [jnp.concatenate([qkv_both[h, :, k * half : (k + 1) * half] for h in sides], 1) for k in range(3)]
    )
    out_part = jnp.concatenate([upo_both[h, :, :half] for h in sides], 1).T
    up_part = jnp.concatenate([upo_both[h, :, half:] for h in sides], 1)
    down_part = jnp.concatenate([down_both[h] for h in sides], 1).T
    base_rate = 1.0 / math.sqrt(SEQ_LEN * lax.axis_size(("chip", "core")))
    slow_rate = MATRIX_RATE * base_rate
    fast_rate = FASTER_RATE * base_rate
    nm_qkv, nw_qkv, na_qkv = advance(w_qkv, m_qkv, a_qkv, qkv_part, slow_rate)
    nm_bqv, nw_bqv, na_bqv = advance(w_bqv, m_bqv, a_bqv, bqv_grad, slow_rate)
    nm_out, nw_out, na_out = advance(w_out, m_out, a_out, out_part, fast_rate)
    nm_up, nw_up, na_up = advance(w_up, m_up, a_up, up_part, slow_rate)
    nm_bup, nw_bup, na_bup = advance(w_bup, m_bup, a_bup, bup_grad, fast_rate)
    nm_down, nw_down, na_down = advance(w_down, m_down, a_down, down_part, slow_rate)
    nm_vec, nw_vec, na_vec = advance(w_vec, m_vec, a_vec, vec_grad, slow_rate)
    return (
        layer_out,
        grad_tokens,
        nm_qkv,
        nw_qkv,
        na_qkv,
        nm_bqv,
        nw_bqv,
        na_bqv,
        nm_out,
        nw_out,
        na_out,
        nm_up,
        nw_up,
        na_up,
        nm_bup,
        nw_bup,
        na_bup,
        nm_down,
        nw_down,
        na_down,
        nm_vec,
        nw_vec,
        na_vec,
    )


def solution(mesh):
    devices = mesh.devices.reshape(-1, 2, 2)
    split_mesh = Mesh(devices, ("chip", "core", "tensor"))
    dp = ("chip", "core")
    row = P(("chip", "core", "tensor"), None)
    deep = P(None, dp, "tensor")
    wide = P("tensor", dp)
    tall = P(dp, "tensor")
    qv = P(None, "tensor")
    unit = P("tensor")
    in_specs = (row, row, P(dp, None)) + (deep,) * 3 + (qv,) * 3 + (wide,) * 3 + (tall,) * 3 + (unit,) * 3 + (wide,) * 3 + (P(),) * 3
    out_specs = (row, row) + in_specs[3:]
    return jax.shard_map(body, mesh=split_mesh, in_specs=in_specs, out_specs=out_specs, check_vma=False)
```

```python
import functools
import math

import jax
import jax.numpy as jnp
from jax import lax
from jax.experimental import pallas as pl
from jax.experimental.pallas import tpu as pltpu
from jax.sharding import Mesh, PartitionSpec as P

HEAD_DIM = 64
SEQ_LEN = 1024


NORM_EPS = 1e-05
MOMENTUM = 0.9
AVERAGE = 0.75
MATRIX_RATE = 0.05
FASTER_RATE = 0.25


def layer_norm(values, gain, shift):
    centred = values - jnp.mean(values, axis=-1, keepdims=True)
    spread = jnp.mean(centred * centred, axis=-1, keepdims=True)
    return centred * lax.rsqrt(spread + NORM_EPS) * gain + shift


def gelu_exact(values):
    return jax.nn.gelu(values, approximate=False)


def advance(weight, moment, average, gradient, step_rate):
    new_moment = MOMENTUM * moment + gradient
    new_weight = weight - step_rate * (gradient + MOMENTUM * new_moment)
    new_average = AVERAGE * average + (1.0 - AVERAGE) * new_weight
    return (new_moment, new_weight, new_average)


NT = (((1,), (1,)), ((), ()))
TN = (((0,), (0,)), ((), ()))
FAR = -1e30


def dot32(left, right, dims=(((1,), (0,)), ((), ()))):
    return lax.dot_general(left, right, dims, preferred_element_type=jnp.float32)


def three_terms(values):
    high = values.astype(jnp.bfloat16).astype(jnp.float32)
    rest = values - high
    middle = rest.astype(jnp.bfloat16).astype(jnp.float32)
    return (high, middle, rest - middle)


def place(lane, terms, other):
    high, middle, low = terms
    return jnp.where(lane == 63, high, jnp.where(lane == 62, middle, jnp.where(lane == 61, low, other)))


def forward_kernel(q_ref, k_ref, v_ref, seg_ref, out_ref, lse_ref, *, block):
    f32, bf16 = jnp.float32, jnp.bfloat16
    rows = q_ref.shape[0]
    lanes = lax.broadcasted_iota(jnp.int32, (rows, 128), 1)
    lower = lanes < HEAD_DIM
    lane = lanes & 63
    same = lane == seg_ref[...]
    q_mark = jnp.where(same, 1.0, 0.0)
    k_mark = jnp.where(same, 0.0, FAR)
    query = q_ref[...].astype(f32)
    keys = k_ref[...].astype(f32) * 0.125
    value = v_ref[...].astype(f32)
    q_heads = [jnp.where(lower, query, q_mark).astype(bf16), jnp.where(lower, q_mark, query).astype(bf16)]
    k_heads = [jnp.where(lower, keys, k_mark).astype(bf16), jnp.where(lower, k_mark, keys).astype(bf16)]
    v_heads = [jnp.where(lower, value, 1.0).astype(bf16), jnp.where(lower, 1.0, value).astype(bf16)]
    low = lower[:block]
    for start in range(0, rows, block):
        parts = []
        for head in range(2):
            scores = dot32(q_heads[head][start : start + block], k_heads[head], NT)
            top = jnp.max(scores, axis=1, keepdims=True)
            weights = jnp.exp(scores - top).astype(bf16)
            parts.append((dot32(weights, v_heads[head]), top))
        (first, top0), (second, top1) = parts
        total = pltpu.roll(jnp.where(low, second, first), HEAD_DIM, 1)
        out_ref[start : start + block, :] = (jnp.where(low, first, second) / total).astype(bf16)
        lse_ref[start : start + block, :] = jnp.where(low, top0, top1) + jnp.log(total)


def backward_kernel(q_ref, k_ref, v_ref, g_ref, o_ref, lse_ref, seg_ref, d_ref, sum_ref, *, block):
    f32, bf16 = jnp.float32, jnp.bfloat16
    rows = q_ref.shape[0]
    lanes = lax.broadcasted_iota(jnp.int32, (rows, 128), 1)
    lower = lanes < HEAD_DIM
    lane = lanes & 63
    same = lane == seg_ref[...]
    query = q_ref[...].astype(f32)
    keys = k_ref[...].astype(f32) * 0.125
    value = v_ref[...].astype(f32)
    grad = g_ref[...].astype(f32)
    lse = pltpu.roll(lse_ref[...], HEAD_DIM, 1)
    q_mark = place(lane, three_terms(-lse), jnp.where(same, 1.0, 0.0))
    k_mark = jnp.where(lane > 60, 1.0, jnp.where(same, 0.0, FAR))
    inner = grad * o_ref[...].astype(f32)
    inner0 = jnp.sum(jnp.where(lower, inner, 0.0), axis=1, keepdims=True)
    inner1 = jnp.sum(jnp.where(lower, 0.0, inner), axis=1, keepdims=True)
    g_mark = place(lane, three_terms(-jnp.where(lower, inner1, inner0)), 0.0)
    v_mark = jnp.where(lane > 60, 1.0, 0.0)

    def heads(values, mark):
        return [jnp.where(lower, values, mark).astype(bf16), jnp.where(lower, mark, values).astype(bf16)]

    q_heads, k_heads = heads(query, q_mark), heads(keys, k_mark)
    v_heads, g_heads = heads(value, v_mark), heads(grad, g_mark)
    q_small = (query * 0.125).astype(bf16)
    k_small = keys.astype(bf16)
    grad16 = g_ref[...]
    low = lower[:block]
    q_grads = [None, None]
    spot = pl.program_id(0) * 128
    places = [pl.ds(pl.multiple_of(k * (d_ref.shape[1] // 3) + spot, 128), 128) for k in range(3)]
    v_sum = jnp.zeros((1, 128), f32)
    for start in range(0, rows, block):
        stop = start + block
        dv, dk = [], []
        for head in range(2):
            probs = jnp.exp(dot32(k_heads[head][start:stop], q_heads[head], NT))
            delta = dot32(v_heads[head][start:stop], g_heads[head], NT)
            dv.append(dot32(probs.astype(bf16), grad16))
            change = (probs * delta).astype(bf16)
            dk.append(dot32(change, q_small))
            part = dot32(change, k_small[start:stop], TN)
            q_grads[head] = part if q_grads[head] is None else q_grads[head] + part
        v_grad = jnp.where(low, dv[0], dv[1])
        v_sum = v_sum + jnp.sum(v_grad, axis=0, keepdims=True)
        d_ref[start:stop, places[1]] = jnp.where(low, dk[0], dk[1]).astype(bf16)
        d_ref[start:stop, places[2]] = v_grad.astype(bf16)
    q_grad = jnp.where(lower, q_grads[0], q_grads[1])
    d_ref[:, places[0]] = q_grad.astype(bf16)
    sum_ref[0:1, :] = jnp.sum(q_grad, axis=0, keepdims=True)
    sum_ref[1:2, :] = v_sum


def part_specs(rows, pairs):
    return [pl.BlockSpec((rows, 128), lambda i, k=k: (0, k * pairs + i)) for k in range(3)]


def attend_forward(packed, seg_col, block=512):
    rows, width = packed.shape
    pairs = width // 384
    flat = pl.BlockSpec((rows, 128), lambda i: (0, i))
    return pl.pallas_call(
        functools.partial(forward_kernel, block=block),
        grid=(pairs,),
        in_specs=part_specs(rows, pairs) + [pl.BlockSpec((rows, 1), lambda i: (0, 0))],
        out_specs=[flat, flat],
        out_shape=[
            jax.ShapeDtypeStruct((rows, pairs * 128), jnp.bfloat16),
            jax.ShapeDtypeStruct((rows, pairs * 128), jnp.float32),
        ],
        compiler_params=pltpu.CompilerParams(vmem_limit_bytes=48 * 2**20),
        name="attend_forward",
    )(packed, packed, packed, seg_col)


def attend_backward(packed, grad, context, lse, seg_col, block=256):
    rows, width = packed.shape
    pairs = width // 384
    flat = pl.BlockSpec((rows, 128), lambda i: (0, i))
    return pl.pallas_call(
        functools.partial(backward_kernel, block=block),
        grid=(pairs,),
        in_specs=part_specs(rows, pairs) + [flat] * 3 + [pl.BlockSpec((rows, 1), lambda i: (0, 0))],
        out_specs=[
            pl.BlockSpec((rows, width), lambda i: (0, 0)),
            pl.BlockSpec((2, 128), lambda i: (0, i)),
        ],
        out_shape=[
            jax.ShapeDtypeStruct((rows, width), jnp.bfloat16),
            jax.ShapeDtypeStruct((2, pairs * 128), jnp.float32),
        ],
        compiler_params=pltpu.CompilerParams(vmem_limit_bytes=48 * 2**20),
        name="attend_backward",
    )(packed, packed, packed, grad, context, lse, seg_col)


CROSS = [(1, 2), (2, 1)]
FLIP = [(0, 1), (1, 0)]


def cross(values):
    return lax.ppermute(values, ("core", "tensor"), CROSS)


def cross_far(values):
    pairs = []
    for chip in range(lax.axis_size("chip")):
        for core in range(2):
            for side in range(2):
                pairs.append((chip * 4 + core * 2 + side, (chip ^ 4) * 4 + side * 2 + core))
    return lax.ppermute(values, ("chip", "core", "tensor"), pairs)


def settle(mine, other):
    return jnp.where(lax.axis_index("core") == lax.axis_index("tensor"), mine, other)


def core_exchange(values):
    return lax.ppermute(values, "core", FLIP)


def y_exchange(values):
    return lax.ppermute(values, "tensor", FLIP)


def chip_exchange(values, mask):
    count = lax.axis_size("chip")
    return lax.ppermute(values, "chip", [(k, k ^ mask) for k in range(count)])


def bits():
    chip = lax.axis_index("chip")
    return (lax.axis_index("tensor"), chip & 1, (chip >> 1) & 1, (chip >> 2) & 1)


STAGES = (
    y_exchange,
    lambda values: chip_exchange(values, 1),
    lambda values: chip_exchange(values, 2),
    lambda values: chip_exchange(values, 4),
)
Y, X, Z1, Z2 = range(4)


def join(mine, other, stage, axis):
    first = bits()[stage] == 0
    return jnp.where(first, jnp.stack([mine, other], axis), jnp.stack([other, mine], axis))


class Gather:
    def __init__(self, held, step=0, mirrored=False):
        self.mirrored = mirrored
        self.rows, self.width = held[0].shape[-2:]
        self.native = lax.axis_size("chip") != 8
        self.flight = ()
        self.held = held
        self.step = step

    def fork(self, width):
        return (
            Gather(tuple(part[..., :width] for part in self.held), self.step),
            Gather(tuple(part[..., width:] for part in self.held), self.step),
        )

    def start(self):
        if self.mirrored:
            far = () if self.native else (cross_far(self.held[0]),)
            self.flight = (cross(self.held[0]),) + far
        elif self.native:
            return
        elif self.step == 0:
            self.flight = (STAGES[Z2](self.held[0]),)
        elif self.step == 1:
            self.flight = (STAGES[Z1](self.held[0]),)
        elif self.step == 2:
            self.flight = (STAGES[X](self.held[0]), STAGES[Y](self.held[1]))
        else:
            self.flight = (STAGES[Y](self.held[0]), STAGES[X](self.held[1]))

    def finish(self):
        if self.mirrored:
            self.held = (settle(self.held[0], self.flight[0]),)
            self.mirrored, self.flight = False, self.flight[1:]
        if self.native:
            return
        if self.step == 0:
            self.held = (join(self.held[0], self.flight[0], Z2, 1),)
        elif self.step == 1:
            self.held = tuple(join(self.held[0][h], self.flight[0][h], Z1, 1) for h in range(2))
        elif self.step == 2:
            left, right = self.held
            self.held = (join(left, self.flight[0], X, 2), join(right, self.flight[1], Y, 2))
        else:
            left, right = self.held
            self.held = (join(left, self.flight[0], Y, 3), join(right, self.flight[1], X, 2))
        self.flight = ()
        self.step += 1

    def result(self):
        if self.native:
            return tuple(lax.all_gather(self.held[0][k], ("chip", "tensor"), axis=0, tiled=True) for k in range(2))
        return tuple(part.reshape(16 * self.rows, self.width) for part in self.held)


class Reduce:
    def __init__(self, left, right):
        self.width = left.shape[-1]
        self.native = lax.axis_size("chip") != 8
        self.held, self.flight = (left, right), ()
        self.step = 0
        if not self.native:
            self.held = tuple(part.reshape(2, 2, 2, 2, -1, self.width) for part in self.held)

    def start(self, order=None, *values):
        if self.native:
            return values
        if self.step == 0:
            plan = ((Y, 3), (X, 2))
        elif self.step == 1:
            plan = ((X, 2), (Y, 2))
        elif self.step == 2:
            plan = ((Z1, self.held[0].ndim - 3),)
        else:
            plan = ((Z2, self.held[0].ndim - 3),)
        self.keep, sends = [], []
        for part, (stage, axis) in zip(self.held, plan):
            bit = bits()[stage]
            self.keep.append(lax.dynamic_index_in_dim(part, bit, axis, keepdims=False))
            sends.append(lax.dynamic_index_in_dim(part, 1 - bit, axis, keepdims=False))
        if order is not None:
            out = order.at(*sends, *values)
            sends, values = out[: len(sends)], out[len(sends) :]
        if self.step == 3:
            self.flight = (cross_far(sends[0]), cross(self.keep[0]))
        else:
            self.flight = tuple(STAGES[stage](send) for send, (stage, _) in zip(sends, plan))
        return values

    def finish(self):
        if self.native:
            return
        if self.step == 3:
            mine = settle(self.keep[0], self.flight[1])
            self.held, self.flight = (mine.astype(jnp.float32) + self.flight[0].astype(jnp.float32),), ()
            return
        total = tuple(
            (mine.astype(jnp.float32) + other.astype(jnp.float32)).astype(jnp.bfloat16)
            for mine, other in zip(self.keep, self.flight)
        )
        self.held = (jnp.stack(total),) if self.step == 1 else total
        self.flight = ()
        self.step += 1

    def result(self):
        if self.native:
            both = jnp.stack(
                [
                    lax.psum_scatter(p, ("chip", "tensor"), scatter_dimension=p.ndim - 2, tiled=True)
                    for p in self.held
                ]
            )
            return settle(both, cross(both)).astype(jnp.float32)
        return self.held[0]


class Sum:
    def __init__(self, values):
        self.native = lax.axis_size("chip") != 8
        if self.native:
            values = lax.psum(values, ("chip", "tensor"))
        self.held, self.flight, self.step = (values,), (), 0

    def start(self):
        if not self.native:
            self.flight = (STAGES[(Z2, Z1, X, Y)[self.step]](self.held[0]),)

    def finish(self):
        if not self.native:
            self.held = (self.held[0] + self.flight[0],)
            self.flight = ()
            self.step += 1


class Order:
    def __init__(self):
        self.now = jnp.zeros((8, 128), jnp.float32)

    def at(self, *values):
        self.now, *values = lax.optimization_barrier((self.now, *values))
        return values

    def follow(self, stream, *values):
        count = len(stream.held)
        out = self.at(*stream.held, *values)
        stream.held = tuple(out[:count])
        return out[count:]

    def arrive(self, streams, *values):
        if not isinstance(streams, tuple):
            streams = (streams,)
        out = self.at(*(part for stream in streams for part in stream.flight), *values)
        for stream in streams:
            count = len(stream.flight)
            stream.flight, out = tuple(out[:count]), out[count:]
            stream.finish()
        return out


def body(
    tokens,
    cotangent,
    segment_ids,
    w_qkv,
    m_qkv,
    a_qkv,
    w_bqv,
    m_bqv,
    a_bqv,
    w_out,
    m_out,
    a_out,
    w_up,
    m_up,
    a_up,
    w_bup,
    m_bup,
    a_bup,
    w_down,
    m_down,
    a_down,
    w_vec,
    m_vec,
    a_vec,
):
    f32, bf16 = jnp.float32, jnp.bfloat16
    core = lax.axis_index("core")
    dev_width = w_bqv.shape[1]
    unit_width = w_bup.shape[0]
    rows = tokens.shape[0]
    half = dev_width // 2
    unit_half = unit_width // 2
    sides = range(2)
    order = Order()

    def pair_dot(lefts, rights, form):
        return sum(jnp.einsum(form, left, right, preferred_element_type=f32) for left, right in zip(lefts, rights))

    def summed(lefts, rights, form):
        away = pair_dot([left[rows:] for left in lefts], rights, form)
        other = core_exchange(away.astype(bf16))
        return pair_dot([left[:rows] for left in lefts], rights, form) + other.astype(f32)

    def full(values):
        return jnp.concatenate([values, core_exchange(values)])

    qkv_shard = w_qkv.astype(bf16)
    qkv_own = jnp.stack(
        [jnp.concatenate([qkv_shard[k, :, h * half : (h + 1) * half] for k in range(3)], 1) for h in sides]
    )
    qkv_own, tokens, cotangent = order.at(qkv_own, tokens, cotangent)
    qkv = Gather((qkv_own,), mirrored=True)
    qkv.start()
    out_shard, up_shard, down_shard = w_out.T.astype(bf16), w_up.astype(bf16), w_down.T.astype(bf16)
    rest = jnp.stack(
        [
            jnp.concatenate(
                [
                    out_shard[:, h * half : (h + 1) * half],
                    up_shard[:, h * unit_half : (h + 1) * unit_half],
                    down_shard[:, h * unit_half : (h + 1) * unit_half],
                ],
                1,
            )
            for h in sides
        ]
    )
    small = jnp.concatenate([w_bqv.reshape(-1), w_bup, segment_ids.reshape(-1).astype(f32)])
    rest, tokens = order.at(rest, tokens)
    rest_other = cross(rest)
    (tokens, small) = order.arrive(qkv, tokens, small)
    qkv.start()
    tok_other = cross(tokens)
    (rest_other, small) = order.arrive(qkv, rest_other, small)
    qkv.start()
    small_other = cross(small)
    upo, down = Gather((settle(rest, rest_other),)).fork(half + unit_half)
    upo.start()
    (tok_other,) = order.arrive((qkv, upo), tok_other)
    qkv.start()
    upo.start()
    tokens = settle(tokens, tok_other)
    tok_far = core_exchange(tokens)
    tok_far, small_other = order.at(tok_far, small_other)
    small = settle(small, small_other)
    b_qv = small[: 2 * dev_width].reshape(2, dev_width)
    b_up = small[2 * dev_width : 2 * dev_width + unit_width]
    segments = small[2 * dev_width + unit_width :].astype(jnp.int32).reshape(1, -1)
    segments = jnp.where(core == 1, jnp.roll(segments, rows, axis=1), segments)
    seg_col = segments.reshape(-1, 1)
    tok_full = jnp.concatenate([tokens, tok_far])
    (tok_full, seg_col, cotangent, *down.held) = order.arrive((upo, qkv), tok_full, seg_col, cotangent, *down.held)
    (tok_full,) = order.follow(upo, tok_full)
    upo.start()
    down.start()
    qkv_w = qkv.result()

    packed, context, logsum = [], [], []
    for h in sides:
        bias = jnp.concatenate(
            [b_qv[0, h * half : (h + 1) * half], jnp.zeros((half,), f32), b_qv[1, h * half : (h + 1) * half]]
        )
        packed.append((jnp.dot(tok_full, qkv_w[h], preferred_element_type=f32) + bias).astype(bf16))
    for h in sides:
        ctx, lse = attend_forward(packed[h], seg_col)
        context.append(ctx)
        logsum.append(lse)
        if h == 0:
            (context[0], packed[1]) = order.arrive((upo, down), context[0], packed[1])
            (packed[1],) = order.follow(upo, packed[1])
            (packed[1],) = order.follow(down, packed[1])
            upo.start()
            down.start()
    context = order.arrive(down, *context)
    context = order.follow(down, *context)
    down.start()
    context = order.arrive(upo, *context)
    uo_w = upo.result()
    out_w = [part[:, :half] for part in uo_w]
    up_w = [part[:, half:] for part in uo_w]

    attended = summed(context, out_w, "ne,de->nd")
    (attended, cotangent) = order.arrive(down, attended, cotangent)
    down.start()
    cot_other = cross(cotangent)
    first_sum = tokens.astype(f32) + attended + w_vec[0]
    hidden, first_pull = jax.vjp(layer_norm, first_sum, w_vec[2], w_vec[3])
    hidden_full = full(hidden.astype(bf16))
    active16, gelu_pulls = [], []
    for h in sides:
        upper = jnp.dot(hidden_full, up_w[h], preferred_element_type=f32) + b_up[h * unit_half : (h + 1) * unit_half]
        active, pull = jax.vjp(gelu_exact, upper)
        active16.append(active.astype(bf16))
        gelu_pulls.append(pull)
    active16 = order.arrive(down, *active16)
    down_w = down.result()
    away = pair_dot([part[rows:] for part in active16], down_w, "nf,df->nd").astype(bf16)
    (away, cot_other) = order.at(away, cot_other)
    cotangent = settle(cotangent, cot_other)
    other = core_exchange(away)
    mixed = pair_dot([part[:rows] for part in active16], down_w, "nf,df->nd") + other.astype(f32)
    second_sum = hidden + mixed + w_vec[1]
    normed, second_pull = jax.vjp(layer_norm, second_sum, w_vec[4], w_vec[5])
    layer_out = normed.astype(bf16)
    second_grad, gain2_grad, shift2_grad = second_pull(cotangent.astype(f32))
    second_far = core_exchange(second_grad.astype(bf16))
    (second_far, layer_out) = order.at(second_far, layer_out)
    out_other = cross(layer_out)
    second_full = jnp.concatenate([second_grad.astype(bf16), second_far])
    down_grads = [jnp.einsum("nd,nf->df", second_full, active16[h], preferred_element_type=f32).astype(bf16) for h in sides]
    (second_full, out_other, *down_grads) = order.at(second_full, out_other, *down_grads)
    down_sum = Reduce(*down_grads)
    down_sum.start()
    upper_grads, upper16, up_grads = [], [], []
    for h in sides:
        active_grad = jnp.einsum("nd,df->nf", second_full, down_w[h], preferred_element_type=f32)
        upper_grads.append(gelu_pulls[h](active_grad)[0])
        upper16.append(upper_grads[h].astype(bf16))
    for h in sides:
        up_grads.append(jnp.einsum("nd,nf->df", hidden_full, upper16[h], preferred_element_type=f32).astype(bf16))
    (upper16[0], upper16[1], *up_grads) = order.arrive(down_sum, *upper16, *up_grads)
    down_sum.start()
    hidden_grad = second_grad + summed(upper16, up_w, "nf,df->nd")
    first_grad, gain1_grad, shift1_grad = first_pull(hidden_grad)
    first_full = full(first_grad.astype(bf16))
    out_grads = [jnp.einsum("nd,ne->de", first_full, context[h], preferred_element_type=f32).astype(bf16) for h in sides]
    uo_grads = [jnp.concatenate([out_grads[h], up_grads[h]], 1) for h in sides]
    (first_full, *uo_grads) = order.at(first_full, *uo_grads)
    upo_sum = Reduce(*uo_grads)
    (first_full,) = upo_sum.start(order, first_full)
    context_grads = [
        jnp.einsum("nd,de->ne", first_full, out_w[h], preferred_element_type=f32).astype(bf16) for h in sides
    ]
    context_grads = order.arrive(down_sum, *context_grads)
    down_sum.start()
    packed16, bias_sums = [None, None], [None, None]
    packed16[0], bias_sums[0] = attend_backward(packed[0], context_grads[0], context[0], logsum[0], seg_col)
    (context_grads[1], packed16[0]) = order.arrive(down_sum, context_grads[1], packed16[0])
    down_sum.start()
    (context_grads[1], packed16[0]) = order.arrive(upo_sum, context_grads[1], packed16[0])
    upo_sum.start()
    vec_local = jnp.stack(
        [
            jnp.sum(first_grad, axis=0),
            jnp.sum(second_grad, axis=0),
            gain1_grad,
            shift1_grad,
            gain2_grad,
            shift2_grad,
        ]
    )
    bup_local = jnp.concatenate([jnp.sum(part, axis=0) for part in upper_grads])
    vec_far = core_exchange(vec_local)
    packed16[1], bias_sums[1] = attend_backward(packed[1], context_grads[1], context[1], logsum[1], seg_col)
    qkv_grads = [jnp.einsum("nd,ne->de", tok_full, packed16[h], preferred_element_type=f32).astype(bf16) for h in sides]
    out = order.arrive((down_sum, upo_sum), vec_far, *packed16, *qkv_grads)
    vec_far, packed16, qkv_grads = out[0], out[1:3], out[3:]
    qkv_sum = Reduce(*qkv_grads)
    qkv_sum.start()
    packed16 = order.follow(upo_sum, *packed16)
    upo_sum.start()
    bqv_local = jnp.concatenate(bias_sums, 1)
    totals = Sum(jnp.concatenate([(vec_local + vec_far).reshape(-1), bqv_local.reshape(-1), bup_local]))
    totals.start()
    down_both = down_sum.result()
    packed16 = order.arrive((upo_sum, totals), *packed16)
    upo_sum.start()
    totals.start()
    (layer_out, out_other, down_both, *packed16) = order.arrive(
        (qkv_sum, totals), layer_out, out_other, down_both, *packed16
    )
    totals.start()
    packed16 = qkv_sum.start(order, *packed16)
    away = pair_dot([part[rows:] for part in packed16], qkv_w, "ne,de->nd")
    grad_far = core_exchange(away.astype(bf16))
    near = pair_dot([part[:rows] for part in packed16], qkv_w, "ne,de->nd")
    grad_tokens = (first_grad + near + grad_far.astype(f32)).astype(bf16)
    layer_out = settle(layer_out, out_other)
    (grad_tokens,) = order.arrive((qkv_sum, totals), grad_tokens)
    qkv_sum.start()
    totals.start()
    grad_other = cross(grad_tokens)
    order.arrive(upo_sum)
    upo_both = upo_sum.result()
    order.arrive(totals)
    vectors = totals.held[0]
    count = vec_local.size
    vec_grad = vectors[:count].reshape(vec_local.shape)
    tail = vectors[count:]
    tail_other = cross(tail)
    order.arrive(qkv_sum)
    qkv_sum.start()
    (tail_other, grad_other) = order.at(tail_other, grad_other)
    order.arrive(qkv_sum)
    qkv_both = qkv_sum.result()
    tail = settle(tail, tail_other)
    bqv_grad = tail[: bqv_local.size].reshape(bqv_local.shape)
    bup_grad = tail[bqv_local.size :]
    grad_tokens = settle(grad_tokens, grad_other)
    (vec_grad,) = order.at(vec_grad)
    vec_grad = vec_grad + order.now[0, 0]
    qkv_part = jnp.stack(
        [jnp.concatenate([qkv_both[h, :, k * half : (k + 1) * half] for h in sides], 1) for k in range(3)]
    )
    out_part = jnp.concatenate([upo_both[h, :, :half] for h in sides], 1).T
    up_part = jnp.concatenate([upo_both[h, :, half:] for h in sides], 1)
    down_part = jnp.concatenate([down_both[h] for h in sides], 1).T
    base_rate = 1.0 / math.sqrt(SEQ_LEN * lax.axis_size(("chip", "core")))
    slow_rate = MATRIX_RATE * base_rate
    fast_rate = FASTER_RATE * base_rate
    nm_qkv, nw_qkv, na_qkv = advance(w_qkv, m_qkv, a_qkv, qkv_part, slow_rate)
    nm_bqv, nw_bqv, na_bqv = advance(w_bqv, m_bqv, a_bqv, bqv_grad, slow_rate)
    nm_out, nw_out, na_out = advance(w_out, m_out, a_out, out_part, fast_rate)
    nm_up, nw_up, na_up = advance(w_up, m_up, a_up, up_part, slow_rate)
    nm_bup, nw_bup, na_bup = advance(w_bup, m_bup, a_bup, bup_grad, fast_rate)
    nm_down, nw_down, na_down = advance(w_down, m_down, a_down, down_part, slow_rate)
    nm_vec, nw_vec, na_vec = advance(w_vec, m_vec, a_vec, vec_grad, slow_rate)
    return (
        layer_out,
        grad_tokens,
        nm_qkv,
        nw_qkv,
        na_qkv,
        nm_bqv,
        nw_bqv,
        na_bqv,
        nm_out,
        nw_out,
        na_out,
        nm_up,
        nw_up,
        na_up,
        nm_bup,
        nw_bup,
        na_bup,
        nm_down,
        nw_down,
        na_down,
        nm_vec,
        nw_vec,
        na_vec,
    )


def solution(mesh):
    devices = mesh.devices.reshape(-1, 2, 2)
    split_mesh = Mesh(devices, ("chip", "core", "tensor"))
    dp = ("chip", "core")
    row = P(("chip", "core", "tensor"), None)
    deep = P(None, dp, "tensor")
    wide = P("tensor", dp)
    tall = P(dp, "tensor")
    qv = P(None, "tensor")
    unit = P("tensor")
    in_specs = (row, row, P(dp, None)) + (deep,) * 3 + (qv,) * 3 + (wide,) * 3 + (tall,) * 3 + (unit,) * 3 + (wide,) * 3 + (P(),) * 3
    out_specs = (row, row) + in_specs[3:]
    return jax.shard_map(body, mesh=split_mesh, in_specs=in_specs, out_specs=out_specs, check_vma=False)
```
